32 devices in a mesh: groups: 2 (over y), pairs: 8 (over z, x), rows: 2 (over core).
Axes of the slice: x: 2, y: 2, z: 4, core: 2. Of those that a mesh axis runs over, the one named last changes fastest.
Arguments:
- first_image: float32 [16, 128, 256], P(('groups', 'pairs'), 'rows'), parts along dimension 0, may hold values from -12 to 12
- second_image: float32 [16, 128, 256], P(('groups', 'pairs'), 'rows'), parts along dimension 0, may hold values from -12 to 12
- prior_motion: float32 [2, 16, 128, 256], P(None, ('groups', 'pairs'), 'rows'), parts along dimension 1, may hold values from -40 to 40
- offsets: int32 [64, 2], replicated, may hold values from -4 to 4, as said below
- pair_epochs: int32 [16, 2], P('groups'), parts along dimension 0, may hold values from 0 to 128, as said below
- pair_slot: int32 [16], P('groups'), parts along dimension 0, may hold values from 0 to 7, each once
Outputs:
- velocity: float32 [2, 128, 4, 16384], P(None, None, ('groups', 'rows'), 'pairs'), parts along dimension 2
- motion: float32 [2, 16, 128, 256], P(None, ('groups', 'pairs'), 'rows'), parts along dimension 1
The draws below stay inside these ranges and needn't reach their ends.
There are 2 independent parts, one for each index of `groups`. The reference program is written for one: setup_inputs(seed, part) draws one part's arguments, and reference() takes and returns one part's arrays. A program takes and returns all parts, laid end to end along the dimension named above; an argument that names none is the same for every part. Nothing has to cross between parts.
Inputs may be any that keep to these rules, and one draw needn't show every extreme that they name: 64 distinct offsets; every offset with a component of magnitude 4 is among them. `pair_epochs`: each row has first < after. `pair_slot`: a permutation of the pairs.
All inputs are finite; a program needn't handle non-finite values. Where the reference program divides by a largest or mean magnitude, that divisor is 1e-20 or more.
Results may differ from the reference program's by a relative error of at most 0.0003.
Values sent between devices are 32-bit elements; how exact they have to be, the bound alone decides.
No kernel may reach another device: no remote copies, remote signals or barrier semaphores. Data moves between devices by JAX's collectives and lax.ppermute only.
A program may use at most 64 MiB of HBM per device.

```python
import jax
import jax.numpy as jnp
from jax import lax

OFFSETS = 64
SEARCH = 4
RADIUS = 4
EPOCHS = 128
RB = 64
W = 256
ITERS = 4
ROUNDS = 2
PAIRS = 8
H = 128
N_ROWS = 2


def image_pair(key):
    subkeys = jax.random.split(jax.random.fold_in(key, 7), 4)
    border = 4
    texture = jax.random.normal(subkeys[0], (PAIRS, H + 2 * border, W + 2 * border), jnp.float32)
    lower_log = jnp.log(0.1)
    upper_log = jnp.log(1.5)
    contrast = jnp.exp(jax.random.uniform(subkeys[1], (PAIRS, H // 8 + 1, W // 8 + 1), jnp.float32, lower_log, upper_log))
    contrast = jnp.repeat(jnp.repeat(contrast, 8, axis=1), 8, axis=2)[:, :H, :W]
    shifts = jax.random.randint(subkeys[2], (PAIRS, 2), -3, 4).astype(jnp.int32)
    moved = jax.vmap(lambda plane, row_shift, col_shift: lax.dynamic_slice(plane, (border + row_shift, border + col_shift), (H, W)))(texture, shifts[:, 0], shifts[:, 1])
    jitter = jax.random.normal(subkeys[3], (PAIRS, H, W), jnp.float32)
    first_window = texture[:, border:border + H, border:border + W] * contrast
    second_view = (moved + 0.5 * jitter) * contrast
    return (jnp.clip(first_window, -12.0, 12.0), jnp.clip(second_view, -12.0, 12.0))


def draw_first_image(key, part):
    return image_pair(key)[0]


def draw_second_image(key, part):
    return image_pair(key)[1]


def draw_prior_motion(key, part):
    subkeys = jax.random.split(jax.random.fold_in(key, 23), 1)
    gentle = jnp.clip(3.0 * jax.random.normal(subkeys[0], (2, PAIRS, H, W), jnp.float32), -9.0, 9.0)
    return gentle


def draw_offsets(key, part):
    subkeys = jax.random.split(jax.random.fold_in(key, 31), 2)
    grid_side = 2 * SEARCH + 1
    item_count = jnp.arange(grid_side * grid_side, dtype=jnp.int32)
    row_part = item_count // grid_side - SEARCH
    col_part = item_count % grid_side - SEARCH
    border_cell = (jnp.abs(row_part) == SEARCH) | (jnp.abs(col_part) == SEARCH)
    ranking = jax.random.permutation(subkeys[0], grid_side * grid_side).astype(jnp.int32)
    priority = jnp.where(border_cell, ranking - grid_side * grid_side, ranking)
    chosen = jnp.argsort(priority, stable=True)[:OFFSETS]
    chosen = chosen[jax.random.permutation(subkeys[1], OFFSETS)]
    return jnp.stack((row_part[chosen], col_part[chosen]), axis=1).astype(jnp.int32)


def draw_pair_epochs(key, part):
    subkeys = jax.random.split(jax.random.fold_in(key, 41), 2)
    starts = jax.random.randint(subkeys[0], (PAIRS,), 0, EPOCHS - 1).astype(jnp.int32)
    lengths_drawn = jax.random.randint(subkeys[1], (PAIRS,), 1, EPOCHS // 4 + 1).astype(jnp.int32)
    starts = starts.at[0].set(0)
    finishes = jnp.minimum(starts + lengths_drawn, EPOCHS)
    finishes = finishes.at[PAIRS - 1].set(EPOCHS)
    return jnp.stack((starts, finishes), axis=1).astype(jnp.int32)


def setup_inputs(seed: int = 0, part: int = 0) -> dict:
    streams_of = jax.random.split(jax.random.key(seed), 7)
    part_splits = jax.random.split(jax.random.fold_in(streams_of[6], part), 7)
    first_image = draw_first_image(jax.random.fold_in(jax.random.fold_in(streams_of[6], part), 71), part)
    second_image = draw_second_image(jax.random.fold_in(jax.random.fold_in(streams_of[6], part), 71), part)
    prior_motion = draw_prior_motion(jax.random.fold_in(jax.random.fold_in(streams_of[6], part), 71), part)
    offsets = draw_offsets(jax.random.fold_in(streams_of[6], 71), part)
    pair_epochs = draw_pair_epochs(jax.random.fold_in(jax.random.fold_in(streams_of[6], part), 71), part)
    pair_slot = jax.random.permutation(part_splits[5], PAIRS).astype(jnp.int32)
    return {"first_image": first_image, "second_image": second_image, "prior_motion": prior_motion, "offsets": offsets, "pair_epochs": pair_epochs, "pair_slot": pair_slot}


SOFTMIN_HEAT = 0.1
PRIOR_STRENGTH = 0.05
PENALTY = 4.0
SPARSITY = 0.4
VARIANCE_FLOOR = 0.05
HIGHEST = lax.Precision.HIGHEST
NEWTON_STEPS = 32

def invert_normal(normal_matrix):
    order = normal_matrix.shape[0]
    identity = jnp.eye(order, dtype=jnp.float32)
    column_bound = jnp.max(lax.optimization_barrier(jnp.sum(jnp.abs(normal_matrix), axis=0)))
    estimate = identity / column_bound
    for step in range(NEWTON_STEPS):
        product = jnp.dot(normal_matrix, estimate, precision=HIGHEST)
        estimate = jnp.dot(estimate, 2.0 * identity - product, precision=HIGHEST)
    return estimate

def box_sum(values):
    window = 2 * RADIUS + 1
    height = values.shape[-2] - 2 * RADIUS
    breadth = values.shape[-1] - 2 * RADIUS
    running = values[..., 0:height, :]
    for position in range(1, window):
        running = running + values[..., position:position + height, :]
    summed = running[..., 0:breadth]
    for position in range(1, window):
        summed = summed + running[..., position:position + breadth]
    return summed / float(window * window)

def correlate(shift_vector, first_padded, second_padded, mean_first, var_first, mean_second_all, square_second_all, height, columns):
    row_start = shift_vector[0] + SEARCH
    col_start = shift_vector[1] + SEARCH
    mean_second = lax.dynamic_slice(mean_second_all, (row_start, col_start), (height, columns))
    square_second = lax.dynamic_slice(square_second_all, (row_start, col_start), (height, columns))
    window_second = lax.dynamic_slice(second_padded, (row_start, col_start), (height + 2 * RADIUS, columns + 2 * RADIUS))
    covariance = box_sum(first_padded * window_second) - mean_first * mean_second
    var_second = square_second - mean_second * mean_second
    return covariance / jnp.sqrt(jnp.maximum(var_first, VARIANCE_FLOOR) * jnp.maximum(var_second, VARIANCE_FLOOR))

def match_pair(first_pair, second_pair, prior_pair, offsets):
    margin = SEARCH + RADIUS
    height, columns = first_pair.shape
    first_padded = jnp.pad(first_pair, RADIUS)
    second_padded = jnp.pad(second_pair, margin)
    mean_first = box_sum(first_padded)
    var_first = box_sum(first_padded * first_padded) - mean_first * mean_first
    mean_second_all = box_sum(second_padded)
    square_second_all = box_sum(second_padded * second_padded)
    cross_correlation = jax.vmap(lambda shift_vector: correlate(shift_vector, first_padded, second_padded, mean_first, var_first, mean_second_all, square_second_all, height, columns))(offsets)
    shifts = offsets.astype(jnp.float32)
    pixel_distance = (shifts[:, 0, None, None] - prior_pair[0]) ** 2 + (shifts[:, 1, None, None] - prior_pair[1]) ** 2
    match_scores = (cross_correlation - PRIOR_STRENGTH * pixel_distance) / SOFTMIN_HEAT
    weights = jax.nn.softmax(match_scores, axis=0)
    return jnp.stack((lax.optimization_barrier(jnp.sum(weights * shifts[:, 0, None, None], axis=0)), lax.optimization_barrier(jnp.sum(weights * shifts[:, 1, None, None], axis=0))))

def build_design(pair_epochs, pair_slot):
    pair_number = jnp.arange(pair_slot.shape[0], dtype=jnp.int32)
    chooser = (pair_slot[:, None] == pair_number[None, :]).astype(jnp.int32)
    starts = lax.optimization_barrier(jnp.sum(chooser * pair_epochs[None, :, 0], axis=1))
    finishes = lax.optimization_barrier(jnp.sum(chooser * pair_epochs[None, :, 1], axis=1))
    epoch_number = jnp.arange(EPOCHS, dtype=jnp.int32)
    inside = (epoch_number[None, :] >= starts[:, None]) & (epoch_number[None, :] < finishes[:, None])
    return inside.astype(jnp.float32)

def reference(first_image, second_image, prior_motion, offsets, pair_epochs, pair_slot):
    design_matrix = build_design(pair_epochs, pair_slot)
    normal_matrix = jnp.dot(design_matrix.T, design_matrix, precision=HIGHEST) + PENALTY * jnp.eye(EPOCHS, dtype=jnp.float32)
    inverse_matrix = invert_normal(normal_matrix)
    threshold = SPARSITY / PENALTY
    sparse = jnp.zeros((2, EPOCHS, H * W), jnp.float32)
    scaled = jnp.zeros((2, EPOCHS, H * W), jnp.float32)
    prior_field = prior_motion
    motion = prior_motion
    for round_number in range(ROUNDS):
        matched = lax.map(lambda members: match_pair(members[0], members[1], members[2], offsets), (first_image, second_image, jnp.moveaxis(prior_field, 1, 0)))
        motion = jnp.moveaxis(matched, 0, 1)
        observed = motion.reshape(2, PAIRS, H * W)
        fixed_part = jnp.einsum('pe,cpn->cen', design_matrix, observed, precision=HIGHEST)
        for iteration in range(ITERS):
            target = fixed_part + PENALTY * (sparse - scaled)
            estimate = jnp.einsum('ef,cfn->cen', inverse_matrix, target, precision=HIGHEST)
            blended = estimate + scaled
            sparse = blended - jnp.clip(blended, -threshold, threshold)
            scaled = blended - sparse
        if round_number + 1 < ROUNDS:
            predicted = jnp.einsum('pe,cen->cpn', design_matrix, sparse, precision=HIGHEST).reshape(2, PAIRS, H, W)
            prior_field = 0.5 * (prior_motion + predicted)
    return (sparse.reshape(2, EPOCHS, N_ROWS, RB * W), motion)
```

```python
import functools

import jax
import jax.numpy as jnp
from jax import lax
from jax.experimental import pallas as pl
from jax.experimental.pallas import tpu as pltpu
from jax.sharding import PartitionSpec as P

OFFSETS = 64
SEARCH = 4
RADIUS = 4
EPOCHS = 128
ITERS = 4
ROUNDS = 2


SOFTMIN_HEAT = 0.1
PRIOR_STRENGTH = 0.05
PENALTY = 4.0
SPARSITY = 0.4
VARIANCE_FLOOR = 0.05
HIGHEST = lax.Precision.HIGHEST
NEWTON_STEPS = 32


def with_halo(cells, sides, width):
    for axis, dim in sides:
        count = lax.axis_size(axis)
        ends = count - 1
        head = lax.slice_in_dim(cells, 0, width, axis=dim)
        tail = lax.slice_in_dim(cells, cells.shape[dim] - width, cells.shape[dim], axis=dim)
        cells = jnp.concatenate(
            [
                lax.ppermute(tail, axis, [(i, (i + 1) % count) for i in range(ends)]),
                cells,
                lax.ppermute(head, axis, [((i + 1) % count, i) for i in range(ends)]),
            ],
            axis=dim,
        )
    return cells


def invert_normal(normal_matrix):
    order = normal_matrix.shape[0]
    identity = jnp.eye(order, dtype=jnp.float32)
    column_bound = jnp.max(jnp.sum(jnp.abs(normal_matrix), axis=0))
    estimate = identity / column_bound
    for step in range(NEWTON_STEPS):
        product = jnp.dot(normal_matrix, estimate, precision=HIGHEST)
        estimate = jnp.dot(estimate, 2.0 * identity - product, precision=HIGHEST)
    return estimate


def box_sum(values):
    window = 2 * RADIUS + 1
    height = values.shape[-2] - 2 * RADIUS
    breadth = values.shape[-1] - 2 * RADIUS
    running = values[..., 0:height, :]
    for position in range(1, window):
        running = running + values[..., position : position + height, :]
    summed = running[..., 0:breadth]
    for position in range(1, window):
        summed = summed + running[..., position : position + breadth]
    return summed / float(window * window)


def correlate(
    shift_vector,
    first_padded,
    second_padded,
    mean_first,
    var_first,
    mean_second_all,
    square_second_all,
    height,
    columns,
):
    row_start = shift_vector[0] + SEARCH
    col_start = shift_vector[1] + SEARCH
    mean_second = lax.dynamic_slice(mean_second_all, (row_start, col_start), (height, columns))
    square_second = lax.dynamic_slice(square_second_all, (row_start, col_start), (height, columns))
    window_second = lax.dynamic_slice(
        second_padded, (row_start, col_start), (height + 2 * RADIUS, columns + 2 * RADIUS)
    )
    covariance = box_sum(first_padded * window_second) - mean_first * mean_second
    var_second = square_second - mean_second * mean_second
    return covariance / jnp.sqrt(
        jnp.maximum(var_first, VARIANCE_FLOOR) * jnp.maximum(var_second, VARIANCE_FLOOR)
    )


def build_design(pair_epochs, pair_slot):
    pair_number = jnp.arange(pair_slot.shape[0], dtype=jnp.int32)
    chooser = (pair_slot[:, None] == pair_number[None, :]).astype(jnp.int32)
    starts = jnp.sum(chooser * pair_epochs[None, :, 0], axis=1)
    finishes = jnp.sum(chooser * pair_epochs[None, :, 1], axis=1)
    epoch_number = jnp.arange(EPOCHS, dtype=jnp.int32)
    inside = (epoch_number[None, :] >= starts[:, None]) & (
        epoch_number[None, :] < finishes[:, None]
    )
    return inside.astype(jnp.float32)


def per_device(first_image, second_image, prior_motion, offsets, pair_epochs, pair_slot):
    band_rows = first_image.shape[1]
    columns = first_image.shape[2]
    margin = SEARCH + RADIUS
    stacked = jnp.concatenate((first_image, second_image), axis=0)
    extended = with_halo(stacked, (("rows", 1),), margin)
    extended = jnp.pad(extended, ((0, 0), (0, 0), (margin, margin)))
    first_padded = extended[
        0, SEARCH : SEARCH + band_rows + 2 * RADIUS, SEARCH : SEARCH + columns + 2 * RADIUS
    ]
    second_padded = extended[1]
    mean_first = box_sum(first_padded)
    var_first = box_sum(first_padded * first_padded) - mean_first * mean_first
    mean_second_all = box_sum(second_padded)
    square_second_all = box_sum(second_padded * second_padded)
    offset_blocks = offsets.reshape(OFFSETS // 8, 8, 2)
    pairs_count = lax.axis_size("pairs")
    pixels = band_rows * columns // pairs_count
    design_matrix = build_design(pair_epochs, pair_slot)
    normal_matrix = jnp.dot(design_matrix.T, design_matrix, precision=HIGHEST) + PENALTY * jnp.eye(
        EPOCHS, dtype=jnp.float32
    )
    inverse_matrix = invert_normal(normal_matrix)
    threshold = SPARSITY / PENALTY
    sparse = jnp.zeros((2, EPOCHS, pixels), jnp.float32)
    scaled = jnp.zeros((2, EPOCHS, pixels), jnp.float32)
    prior_band = prior_motion[:, 0]
    motion = prior_band
    for round_number in range(ROUNDS):

        def block_step(state_now, offset_block):
            running_max, weight_sum, sum_rows, sum_cols = state_now
            cross_correlation = jax.vmap(
                lambda shift_vector: correlate(
                    shift_vector,
                    first_padded,
                    second_padded,
                    mean_first,
                    var_first,
                    mean_second_all,
                    square_second_all,
                    band_rows,
                    columns,
                )
            )(offset_block)
            shifts = offset_block.astype(jnp.float32)
            pixel_distance = (shifts[:, 0, None, None] - prior_band[0]) ** 2 + (
                shifts[:, 1, None, None] - prior_band[1]
            ) ** 2
            match_scores = (cross_correlation - PRIOR_STRENGTH * pixel_distance) / SOFTMIN_HEAT
            new_max = jnp.maximum(running_max, jnp.max(match_scores, axis=0))
            rescale = jnp.exp(running_max - new_max)
            weights = jnp.exp(match_scores - new_max)
            weight_sum = weight_sum * rescale + jnp.sum(weights, axis=0)
            sum_rows = sum_rows * rescale + jnp.sum(weights * shifts[:, 0, None, None], axis=0)
            sum_cols = sum_cols * rescale + jnp.sum(weights * shifts[:, 1, None, None], axis=0)
            return ((new_max, weight_sum, sum_rows, sum_cols), None)

        zeros_band = jnp.zeros((band_rows, columns), jnp.float32)
        initial = (
            jnp.full((band_rows, columns), -jnp.inf, jnp.float32),
            zeros_band,
            zeros_band,
            zeros_band,
        )
        (running_max, weight_sum, sum_rows, sum_cols), unused = lax.scan(
            block_step, initial, offset_blocks
        )
        motion = jnp.stack((sum_rows / weight_sum, sum_cols / weight_sum))
        outgoing = motion.reshape(2, 1, pairs_count, pixels)
        arrived = lax.all_to_all(outgoing, "pairs", split_axis=2, concat_axis=1, tiled=True)
        observed = arrived.reshape(2, arrived.shape[1], pixels)
        fixed_part = jnp.einsum("pe,cpn->cen", design_matrix, observed, precision=HIGHEST)
        for iteration in range(ITERS):
            target = fixed_part + PENALTY * (sparse - scaled)
            estimate = jnp.einsum("ef,cfn->cen", inverse_matrix, target, precision=HIGHEST)
            blended = estimate + scaled
            sparse = blended - jnp.clip(blended, -threshold, threshold)
            scaled = blended - sparse
        if round_number + 1 < ROUNDS:
            predicted = jnp.einsum("pe,cen->cpn", design_matrix, sparse, precision=HIGHEST)
            predicted = predicted.reshape(2, predicted.shape[1], 1, pixels)
            returned = lax.all_to_all(predicted, "pairs", split_axis=1, concat_axis=2, tiled=True)
            prior_band = 0.5 * (prior_motion[:, 0] + returned.reshape(2, band_rows, columns))
    return (sparse[:, :, None, :], motion[:, None])


LANES = 128
SUBLANES = 8
GROUP = 4
SPAN = 2 * SEARCH + 1
WINDOW = 2 * RADIUS + 1
SCALE = 1.4426950408889634 / SOFTMIN_HEAT


def pack_kernel(first, second, prior, edge, out, ext_first, ext_second, *, rows_axis, strip, blocks):
    margin = SEARCH + RADIUS
    band = first.shape[0]
    here = lax.axis_index(rows_axis)
    count = lax.axis_size(rows_axis)
    none = jnp.zeros((margin, first.shape[1]), jnp.float32)
    for slot, (source, ext) in enumerate(((first, ext_first), (second, ext_second))):
        got = edge[slot]
        ext[0:margin, :] = jnp.where(here > 0, got, none)
        ext[margin : margin + band, :] = source[...]
        ext[margin + band : band + 2 * margin, :] = jnp.where(here < count - 1, got, none)
    tiles = first.shape[1] // LANES
    per = 5 * strip + 2 * RADIUS + 2 * margin - strip
    tall = strip + 2 * RADIUS
    taller = strip + 2 * margin
    for block in range(blocks):
        for tile in range(tiles):
            lanes = slice(tile * LANES, (tile + 1) * LANES)
            at = (block * tiles + tile) * per
            top = block * strip
            out[at : at + tall, :] = ext_first[top + SEARCH : top + SEARCH + tall, lanes]
            at += tall
            out[at : at + taller, :] = ext_second[top : top + taller, lanes]
            at += taller
            out[at : at + strip, :] = prior[0, top : top + strip, lanes]
            at += strip
            out[at : at + strip, :] = prior[1, top : top + strip, lanes]


def window_sums(rows):
    count = len(rows)
    twos = [rows[a] + rows[a + 1] for a in range(count - 1)]
    fours = [twos[a] + twos[a + 2] for a in range(count - 3)]
    eights = [fours[a] + fours[a + 4] for a in range(count - 7)]
    return [eights[a] + rows[a + 8] for a in range(count - 8)]


def store_split(parts, at, lanes, upper, lower):
    value = jnp.concatenate((upper, lower), axis=0)
    high = value.astype(jnp.bfloat16)
    rest = value - high.astype(jnp.float32)
    mid = rest.astype(jnp.bfloat16)
    low = (rest - mid.astype(jnp.float32)).astype(jnp.bfloat16)
    for part, piece in enumerate((high, mid, low)):
        parts[part, at : at + 2 * SUBLANES, lanes] = piece


def split_dot(parts, right):
    total = jnp.dot(parts[0], right, preferred_element_type=jnp.float32)
    total = total + jnp.dot(parts[1], right, preferred_element_type=jnp.float32)
    return total + jnp.dot(parts[2], right, preferred_element_type=jnp.float32)


def lane_shift(tiles, edge, shift, lane):
    if shift == 0:
        return tiles
    rolled = [pltpu.roll(tile, (-shift) % LANES, 1) for tile in tiles]
    outer = jnp.zeros_like(tiles[0]) if edge is None else pltpu.roll(edge, (-shift) % LANES, 1)
    if shift > 0:
        keep = lane < LANES - shift
        following = rolled[1:] + [outer]
        return [jnp.where(keep, own, other) for own, other in zip(rolled, following)]
    keep = lane >= -shift
    before = [outer] + rolled[:-1]
    return [jnp.where(keep, own, other) for own, other in zip(rolled, before)]


def track_kernel(
    offsets,
    pair_epochs,
    pair_slot,
    data,
    velocity,
    motion,
    band,
    stat_parts,
    parts,
    first,
    second,
    mean_first,
    scale_first,
    mean_second,
    scale_second,
    table,
    prior,
    matched,
    predicted,
    sparse,
    spread,
    running,
    steps,
    inverse,
    lengths,
    order,
    bounds,
):
    strip = SUBLANES
    margin = SEARCH + RADIUS
    tall = strip + 2 * RADIUS
    taller = strip + 2 * margin
    per = tall + taller + 2 * strip
    wide = strip + 2 * SEARCH
    area = float(WINDOW * WINDOW)
    count = pair_slot.shape[0]
    columns = band.shape[0]
    tiles = columns // LANES
    cells = strip * tiles
    lane = lax.broadcasted_iota(jnp.int32, (SUBLANES, LANES), 1)

    tap = lax.broadcasted_iota(jnp.int32, band.shape, 0)
    column = lax.broadcasted_iota(jnp.int32, band.shape, 1)
    centre = jnp.where(column < columns + LANES // 2, column, column - columns - LANES)
    band[...] = jnp.where(jnp.abs(tap - centre) <= RADIUS, 1.0, 0.0).astype(jnp.bfloat16)

    def fetch(row, tile):
        return data[pl.ds(tile * per + row, SUBLANES, stride=tiles * per), :]

    for component in range(2):
        for row in range(strip):
            for tile in range(tiles):
                prior[component * cells + row * tiles + tile] = fetch(tall + taller + component * strip + row, tile)

    for tile in range(tiles):
        lanes = slice(tile * LANES, (tile + 1) * LANES)
        rows = [fetch(row, tile) for row in range(tall)]
        for row in range(tall):
            first[row * tiles + tile] = rows[row]
        at = 0
        for values in (rows, [row * row for row in rows]):
            sums = window_sums(values)
            for row in range(0, strip, 2):
                store_split(stat_parts, at, lanes, sums[row], sums[row + 1])
                at += 2 * SUBLANES
        rows = [fetch(tall + row, tile) for row in range(taller)]
        for values in (rows, [row * row for row in rows]):
            sums = window_sums(values)
            for row in range(0, wide, 2):
                store_split(stat_parts, at, lanes, sums[row], sums[row + 1])
                at += 2 * SUBLANES
    for row in range(taller):
        pieces = [fetch(tall + row, tile) for tile in range(tiles)]
        for shift in range(-SEARCH, SEARCH + 1):
            moved = lane_shift(pieces, None, shift, lane)
            for tile in range(tiles):
                second[((shift + SEARCH) * taller + row) * tiles + tile] = moved[tile]
    sums = split_dot(stat_parts, band[...])
    for row in range(strip):
        for tile in range(tiles):
            lanes = slice(tile * LANES, (tile + 1) * LANES)
            total = sums[row * SUBLANES : (row + 1) * SUBLANES, lanes]
            squares = sums[(strip + row) * SUBLANES : (strip + row + 1) * SUBLANES, lanes] / area
            mean = total / area
            mean_first[row * tiles + tile] = total
            scale_first[row * tiles + tile] = lax.rsqrt(
                jnp.maximum(squares - mean * mean, VARIANCE_FLOOR)
            ) * (SCALE / area)
    for row in range(wide):
        means, scales = [], []
        for tile in range(tiles + 1):
            lanes = slice(tile * LANES, (tile + 1) * LANES)
            at = (2 * strip + row) * SUBLANES
            mean = sums[at : at + SUBLANES, lanes] / area
            at = (2 * strip + wide + row) * SUBLANES
            squares = sums[at : at + SUBLANES, lanes] / area
            means.append(mean)
            scales.append(lax.rsqrt(jnp.maximum(squares - mean * mean, VARIANCE_FLOOR)))
        for shift in range(-SEARCH, SEARCH + 1):
            for values, held in ((means, mean_second), (scales, scale_second)):
                moved = lane_shift(values[:tiles], values[tiles], shift, lane)
                for tile in range(tiles):
                    held[((shift + SEARCH) * wide + row) * tiles + tile] = moved[tile]

    nothing = jnp.zeros((SUBLANES, LANES), jnp.float32)

    def clear(index, carry):
        table[index] = nothing
        return carry

    lax.fori_loop(0, SPAN * SPAN * cells, clear, 0, unroll=8)

    def offset_group(group, carry):
        places = []
        for member in range(GROUP):
            row_shift = offsets[group * GROUP + member, 0] + SEARCH
            column_shift = offsets[group * GROUP + member, 1] + SEARCH
            places.append((row_shift, column_shift))
            at_second = (column_shift * taller + row_shift) * tiles
            for tile in range(tiles):
                lanes = slice(tile * LANES, (tile + 1) * LANES)
                products = [
                    first[row * tiles + tile] * second[at_second + row * tiles + tile]
                    for row in range(tall)
                ]
                sums = window_sums(products)
                for row in range(0, strip, 2):
                    at = member * strip * SUBLANES + row * SUBLANES
                    store_split(parts, at, lanes, sums[row], sums[row + 1])
        crossed = split_dot(parts, band[:, 0:columns])
        for member in range(GROUP):
            row_shift, column_shift = places[member]
            at_second = (column_shift * wide + row_shift) * tiles
            at_table = (column_shift * SPAN + row_shift) * cells
            for row in range(strip):
                for tile in range(tiles):
                    at = (member * strip + row) * SUBLANES
                    cell = row * tiles + tile
                    total = crossed[at : at + SUBLANES, tile * LANES : (tile + 1) * LANES]
                    covariance = total - mean_first[cell] * mean_second[at_second + cell]
                    scaled = covariance * (scale_first[cell] * scale_second[at_second + cell])
                    table[at_table + cell] = jnp.exp2(scaled)
        return carry

    lax.fori_loop(0, offsets.shape[0] // GROUP, offset_group, 0)

    ends = [pair_epochs[pair_slot[j], 0] for j in range(count)]
    ends += [pair_epochs[pair_slot[j], 1] for j in range(count)]
    ranks = [jnp.int32(0)] * (2 * count)
    for a in range(2 * count):
        for b in range(a + 1, 2 * count):
            ahead = (ends[a] <= ends[b]).astype(jnp.int32)
            ranks[b] = ranks[b] + ahead
            ranks[a] = ranks[a] + (1 - ahead)
    for a in range(2 * count):
        order[ranks[a]] = a
        bounds[ranks[a]] = ends[a]
    segments = 2 * count - 1
    for s in range(segments):
        lengths[s] = jnp.full((SUBLANES, LANES), (bounds[s + 1] - bounds[s]).astype(jnp.float32))

    gram = [[None] * count for _ in range(count)]
    for a in range(count):
        for b in range(a, count):
            shared = jnp.minimum(ends[count + a], ends[count + b]) - jnp.maximum(ends[a], ends[b])
            value = jnp.maximum(shared, 0).astype(jnp.float32) + (PENALTY if a == b else 0.0)
            gram[a][b] = gram[b][a] = jnp.full((SUBLANES, LANES), value)
    for k in range(count):
        pivot = 1.0 / gram[k][k]
        scaled = [gram[k][b] * pivot for b in range(count)]
        for a in range(count):
            if a == k:
                continue
            factor = gram[a][k]
            for b in range(count):
                if b != k:
                    gram[a][b] = gram[a][b] - factor * scaled[b]
            gram[a][k] = -(factor * pivot)
        for b in range(count):
            gram[k][b] = scaled[b]
        gram[k][k] = pivot
    for a in range(count):
        for b in range(count):
            inverse[a * count + b] = gram[a][b]

    halves = cells // SUBLANES
    groups = 2 * halves
    threshold = SPARSITY / PENALTY

    def match(first_guess):
        def pixel_tile(cell, carry):
            guess = []
            for component in range(2):
                value = prior[component * cells + cell]
                if not first_guess:
                    at = pl.multiple_of((component * cells + cell) * SUBLANES, SUBLANES)
                    value = 0.5 * (value + predicted[pl.ds(at, SUBLANES), :])
                guess.append(value)
            factors = []
            for value in guess:
                nearest = jnp.clip(jnp.round(value), -float(SEARCH), float(SEARCH))
                peak = nearest * value - 0.5 * nearest * nearest
                factors.append(
                    [
                        jnp.exp(value * float(shift) - (peak + 0.5 * shift * shift))
                        for shift in range(-SEARCH, SEARCH + 1)
                    ]
                )
            weight = row_moment = column_moment = None
            for column_shift in range(SPAN):
                part = moment = None
                for row_shift in range(SPAN):
                    term = factors[0][row_shift] * table[(column_shift * SPAN + row_shift) * cells + cell]
                    lever = term * float(row_shift - SEARCH)
                    part = term if part is None else part + term
                    if row_shift != SEARCH:
                        moment = lever if moment is None else moment + lever
                factor = factors[1][column_shift]
                part = part * factor
                moment = moment * factor
                lever = part * float(column_shift - SEARCH)
                weight = part if weight is None else weight + part
                row_moment = moment if row_moment is None else row_moment + moment
                column_moment = lever if column_moment is None else column_moment + lever
            share = 1.0 / weight
            for component, value in enumerate((row_moment, column_moment)):
                at = pl.multiple_of((component * cells + cell) * SUBLANES, SUBLANES)
                matched[pl.ds(at, SUBLANES), :] = value * share
            return carry

        lax.fori_loop(0, cells, pixel_tile, 0)

    def across(group, j):
        return pl.ds(group * SUBLANES * SUBLANES + j, SUBLANES, stride=SUBLANES)

    starts = ranks[:count]
    finishes = ranks[count:]

    def invert():
        def iterate(iteration, carry):
            for group in range(groups):
                total = nothing
                running[group, 0] = total
                for s in range(segments):
                    total = total + lengths[s] * spread[group, s]
                    running[group, s + 1] = total
                residual = [
                    matched[across(group, j), :]
                    - (running[group, finishes[j]] - running[group, starts[j]])
                    for j in range(count)
                ]
                for a in range(count):
                    step = inverse[a * count] * residual[0]
                    for b in range(1, count):
                        step = step + inverse[a * count + b] * residual[b]
                    steps[group, a] = step
                    steps[group, count + a] = -step
                level = nothing
                for s in range(segments):
                    level = level + steps[group, order[s]]
                    blended = sparse[group, s + 1] + level
                    scaled = jnp.clip(blended, -threshold, threshold)
                    shrunk = blended - scaled
                    sparse[group, s + 1] = shrunk
                    spread[group, s] = shrunk - scaled
            return carry

        lax.fori_loop(0, ITERS, iterate, 0)

    for group in range(groups):
        for s in range(segments):
            spread[group, s] = nothing
        for s in range(segments + 2):
            sparse[group, s] = nothing
    for round_number in range(ROUNDS):
        match(round_number == 0)
        invert()
        if round_number + 1 < ROUNDS:
            for group in range(groups):
                total = nothing
                running[group, 0] = total
                for s in range(segments):
                    total = total + lengths[s] * sparse[group, s + 1]
                    running[group, s + 1] = total
                for j in range(count):
                    predicted[across(group, j), :] = (
                        running[group, finishes[j]] - running[group, starts[j]]
                    )

    for j in range(count):
        for component in range(2):
            for tile in range(tiles):
                at = (component * cells + tile) * SUBLANES + j
                motion[j, component, :, tile * LANES : (tile + 1) * LANES] = matched[
                    pl.ds(at, SUBLANES, stride=tiles * SUBLANES), :
                ]

    def fill(low, high, s):
        held = [sparse[group, s] for group in range(groups)]

        def one(epoch, carry):
            for group in range(groups):
                half = group % halves
                velocity[group // halves, epoch, half * SUBLANES : (half + 1) * SUBLANES, :] = held[group]
            return carry

        lax.fori_loop(low, high, one, 0)

    epochs = velocity.shape[1]
    fill(0, bounds[0], 0)
    for s in range(segments):
        fill(bounds[s], bounds[s + 1], s + 1)
    fill(bounds[segments], epochs, segments + 1)


def by_strips(first_image, second_image, prior_motion, offsets, pair_epochs, pair_slot):
    band_rows, columns = first_image.shape[1:]
    margin = SEARCH + RADIUS
    count = lax.axis_size("pairs")
    strip = band_rows // count
    tiles = columns // LANES
    cells = strip * tiles
    tall = strip + 2 * RADIUS
    taller = strip + 2 * margin
    wide = strip + 2 * SEARCH
    per = tall + taller + 2 * strip
    here = lax.axis_index("rows")
    start = jnp.where(here == 0, band_rows - margin, 0)
    images = (first_image[0], second_image[0])
    edge = jnp.stack([lax.dynamic_slice(image, (start, 0), (margin, columns)) for image in images])
    edge = lax.ppermute(edge, "rows", [(0, 1), (1, 0)])
    packed = pl.pallas_call(
        functools.partial(pack_kernel, rows_axis="rows", strip=strip, blocks=count),
        out_shape=jax.ShapeDtypeStruct((count * tiles * per, LANES), jnp.float32),
        scratch_shapes=[pltpu.VMEM((band_rows + 2 * margin, columns), jnp.float32)] * 2,
    )(first_image[0], second_image[0], prior_motion[:, 0], edge)
    arrived = lax.all_to_all(packed, "pairs", split_axis=0, concat_axis=0, tiled=True)
    tile = lambda *lead: pltpu.VMEM((*lead, SUBLANES, LANES), jnp.float32)
    flat = lambda rows: pltpu.VMEM((rows * SUBLANES, LANES), jnp.float32)
    groups = 2 * cells // SUBLANES
    stat_rows = (2 * strip + 2 * wide) * SUBLANES
    smem = pl.BlockSpec(memory_space=pltpu.SMEM)
    vmem = pl.BlockSpec(memory_space=pltpu.VMEM)
    velocity, motion = pl.pallas_call(
        track_kernel,
        out_shape=(
            jax.ShapeDtypeStruct((2, EPOCHS, cells, LANES), jnp.float32),
            jax.ShapeDtypeStruct((count, 2, strip, columns), jnp.float32),
        ),
        in_specs=[smem, smem, smem, vmem],
        out_specs=(vmem, vmem),
        scratch_shapes=[
            pltpu.VMEM((columns, columns + LANES), jnp.bfloat16),
            pltpu.VMEM((3, stat_rows, columns), jnp.bfloat16),
            pltpu.VMEM((3, GROUP * strip * SUBLANES, columns), jnp.bfloat16),
            tile(tall * tiles),
            tile(SPAN * taller * tiles),
            tile(cells),
            tile(cells),
            tile(SPAN * wide * tiles),
            tile(SPAN * wide * tiles),
            tile(SPAN * SPAN * cells),
            tile(2 * cells),
            flat(2 * cells),
            flat(2 * cells),
            tile(groups, 2 * count + 1),
            tile(groups, 2 * count - 1),
            tile(groups, 2 * count),
            tile(groups, 2 * count),
            tile(count * count),
            tile(2 * count - 1),
            pltpu.SMEM((2 * count,), jnp.int32),
            pltpu.SMEM((2 * count,), jnp.int32),
        ],
        compiler_params=pltpu.CompilerParams(vmem_limit_bytes=48 * 1024 * 1024),
    )(offsets, pair_epochs, pair_slot, arrived)
    returned = lax.all_to_all(motion, "pairs", split_axis=0, concat_axis=0, tiled=True)
    returned = jnp.moveaxis(returned, 0, 1).reshape(2, 1, band_rows, columns)
    return (velocity.reshape(2, EPOCHS, 1, strip * columns), returned)


def per_device_any(first_image, second_image, *rest):
    band_rows, columns = first_image.shape[1:]
    count = lax.axis_size("pairs")
    strips = (
        count == SUBLANES
        and band_rows == count * SUBLANES
        and columns == 2 * LANES
        and lax.axis_size("rows") == 2
        and rest[1].shape[0] % GROUP == 0
    )
    plan = by_strips if strips else per_device
    return plan(first_image, second_image, *rest)


def solution(mesh):
    placed = (
        P(("groups", "pairs"), "rows", None),
        P(("groups", "pairs"), "rows", None),
        P(None, ("groups", "pairs"), "rows", None),
        P(),
        P("groups", None),
        P("groups"),
    )
    return jax.shard_map(
        per_device_any,
        mesh=mesh,
        in_specs=placed,
        out_specs=(
            P(None, None, ("groups", "rows"), "pairs"),
            P(None, ("groups", "pairs"), "rows", None),
        ),
        check_vma=False,
    )
```

```python
import functools

import jax
import jax.numpy as jnp
from jax import lax
from jax.experimental import pallas as pl
from jax.experimental.pallas import tpu as pltpu
from jax.sharding import PartitionSpec as P

OFFSETS = 64
SEARCH = 4
RADIUS = 4
EPOCHS = 128
ITERS = 4
ROUNDS = 2


SOFTMIN_HEAT = 0.1
PRIOR_STRENGTH = 0.05
PENALTY = 4.0
SPARSITY = 0.4
VARIANCE_FLOOR = 0.05
HIGHEST = lax.Precision.HIGHEST
NEWTON_STEPS = 32


def with_halo(cells, sides, width):
    for axis, dim in sides:
        count = lax.axis_size(axis)
        ends = count - 1
        head = lax.slice_in_dim(cells, 0, width, axis=dim)
        tail = lax.slice_in_dim(cells, cells.shape[dim] - width, cells.shape[dim], axis=dim)
        cells = jnp.concatenate(
            [
                lax.ppermute(tail, axis, [(i, (i + 1) % count) for i in range(ends)]),
                cells,
                lax.ppermute(head, axis, [((i + 1) % count, i) for i in range(ends)]),
            ],
            axis=dim,
        )
    return cells


def invert_normal(normal_matrix):
    order = normal_matrix.shape[0]
    identity = jnp.eye(order, dtype=jnp.float32)
    column_bound = jnp.max(jnp.sum(jnp.abs(normal_matrix), axis=0))
    estimate = identity / column_bound
    for step in range(NEWTON_STEPS):
        product = jnp.dot(normal_matrix, estimate, precision=HIGHEST)
        estimate = jnp.dot(estimate, 2.0 * identity - product, precision=HIGHEST)
    return estimate


def box_sum(values):
    window = 2 * RADIUS + 1
    height = values.shape[-2] - 2 * RADIUS
    breadth = values.shape[-1] - 2 * RADIUS
    running = values[..., 0:height, :]
    for position in range(1, window):
        running = running + values[..., position : position + height, :]
    summed = running[..., 0:breadth]
    for position in range(1, window):
        summed = summed + running[..., position : position + breadth]
    return summed / float(window * window)


def correlate(
    shift_vector,
    first_padded,
    second_padded,
    mean_first,
    var_first,
    mean_second_all,
    square_second_all,
    height,
    columns,
):
    row_start = shift_vector[0] + SEARCH
    col_start = shift_vector[1] + SEARCH
    mean_second = lax.dynamic_slice(mean_second_all, (row_start, col_start), (height, columns))
    square_second = lax.dynamic_slice(square_second_all, (row_start, col_start), (height, columns))
    window_second = lax.dynamic_slice(
        second_padded, (row_start, col_start), (height + 2 * RADIUS, columns + 2 * RADIUS)
    )
    covariance = box_sum(first_padded * window_second) - mean_first * mean_second
    var_second = square_second - mean_second * mean_second
    return covariance / jnp.sqrt(
        jnp.maximum(var_first, VARIANCE_FLOOR) * jnp.maximum(var_second, VARIANCE_FLOOR)
    )


def build_design(pair_epochs, pair_slot):
    pair_number = jnp.arange(pair_slot.shape[0], dtype=jnp.int32)
    chooser = (pair_slot[:, None] == pair_number[None, :]).astype(jnp.int32)
    starts = jnp.sum(chooser * pair_epochs[None, :, 0], axis=1)
    finishes = jnp.sum(chooser * pair_epochs[None, :, 1], axis=1)
    epoch_number = jnp.arange(EPOCHS, dtype=jnp.int32)
    inside = (epoch_number[None, :] >= starts[:, None]) & (
        epoch_number[None, :] < finishes[:, None]
    )
    return inside.astype(jnp.float32)


def per_device(first_image, second_image, prior_motion, offsets, pair_epochs, pair_slot):
    band_rows = first_image.shape[1]
    columns = first_image.shape[2]
    margin = SEARCH + RADIUS
    stacked = jnp.concatenate((first_image, second_image), axis=0)
    extended = with_halo(stacked, (("rows", 1),), margin)
    extended = jnp.pad(extended, ((0, 0), (0, 0), (margin, margin)))
    first_padded = extended[
        0, SEARCH : SEARCH + band_rows + 2 * RADIUS, SEARCH : SEARCH + columns + 2 * RADIUS
    ]
    second_padded = extended[1]
    mean_first = box_sum(first_padded)
    var_first = box_sum(first_padded * first_padded) - mean_first * mean_first
    mean_second_all = box_sum(second_padded)
    square_second_all = box_sum(second_padded * second_padded)
    offset_blocks = offsets.reshape(OFFSETS // 8, 8, 2)
    pairs_count = lax.axis_size("pairs")
    pixels = band_rows * columns // pairs_count
    design_matrix = build_design(pair_epochs, pair_slot)
    normal_matrix = jnp.dot(design_matrix.T, design_matrix, precision=HIGHEST) + PENALTY * jnp.eye(
        EPOCHS, dtype=jnp.float32
    )
    inverse_matrix = invert_normal(normal_matrix)
    threshold = SPARSITY / PENALTY
    sparse = jnp.zeros((2, EPOCHS, pixels), jnp.float32)
    scaled = jnp.zeros((2, EPOCHS, pixels), jnp.float32)
    prior_band = prior_motion[:, 0]
    motion = prior_band
    for round_number in range(ROUNDS):

        def block_step(state_now, offset_block):
            running_max, weight_sum, sum_rows, sum_cols = state_now
            cross_correlation = jax.vmap(
                lambda shift_vector: correlate(
                    shift_vector,
                    first_padded,
                    second_padded,
                    mean_first,
                    var_first,
                    mean_second_all,
                    square_second_all,
                    band_rows,
                    columns,
                )
            )(offset_block)
            shifts = offset_block.astype(jnp.float32)
            pixel_distance = (shifts[:, 0, None, None] - prior_band[0]) ** 2 + (
                shifts[:, 1, None, None] - prior_band[1]
            ) ** 2
            match_scores = (cross_correlation - PRIOR_STRENGTH * pixel_distance) / SOFTMIN_HEAT
            new_max = jnp.maximum(running_max, jnp.max(match_scores, axis=0))
            rescale = jnp.exp(running_max - new_max)
            weights = jnp.exp(match_scores - new_max)
            weight_sum = weight_sum * rescale + jnp.sum(weights, axis=0)
            sum_rows = sum_rows * rescale + jnp.sum(weights * shifts[:, 0, None, None], axis=0)
            sum_cols = sum_cols * rescale + jnp.sum(weights * shifts[:, 1, None, None], axis=0)
            return ((new_max, weight_sum, sum_rows, sum_cols), None)

        zeros_band = jnp.zeros((band_rows, columns), jnp.float32)
        initial = (
            jnp.full((band_rows, columns), -jnp.inf, jnp.float32),
            zeros_band,
            zeros_band,
            zeros_band,
        )
        (running_max, weight_sum, sum_rows, sum_cols), unused = lax.scan(
            block_step, initial, offset_blocks
        )
        motion = jnp.stack((sum_rows / weight_sum, sum_cols / weight_sum))
        outgoing = motion.reshape(2, 1, pairs_count, pixels)
        arrived = lax.all_to_all(outgoing, "pairs", split_axis=2, concat_axis=1, tiled=True)
        observed = arrived.reshape(2, arrived.shape[1], pixels)
        fixed_part = jnp.einsum("pe,cpn->cen", design_matrix, observed, precision=HIGHEST)
        for iteration in range(ITERS):
            target = fixed_part + PENALTY * (sparse - scaled)
            estimate = jnp.einsum("ef,cfn->cen", inverse_matrix, target, precision=HIGHEST)
            blended = estimate + scaled
            sparse = blended - jnp.clip(blended, -threshold, threshold)
            scaled = blended - sparse
        if round_number + 1 < ROUNDS:
            predicted = jnp.einsum("pe,cen->cpn", design_matrix, sparse, precision=HIGHEST)
            predicted = predicted.reshape(2, predicted.shape[1], 1, pixels)
            returned = lax.all_to_all(predicted, "pairs", split_axis=1, concat_axis=2, tiled=True)
            prior_band = 0.5 * (prior_motion[:, 0] + returned.reshape(2, band_rows, columns))
    return (sparse[:, :, None, :], motion[:, None])


LANES = 128
SUBLANES = 8
GROUP = 4
SPAN = 2 * SEARCH + 1
WINDOW = 2 * RADIUS + 1
SCALE = 1.4426950408889634 / SOFTMIN_HEAT


def strip_rows(strip):
    tall = strip + 2 * RADIUS
    taller = strip + 2 * (SEARCH + RADIUS)
    return tall, taller, tall + taller + 2 * strip


def pack_kernel(first_in, second_in, prior_in, out, first, second, prior, arrivals):
    copies = [
        pltpu.make_async_copy(source, target, arrivals.at[k])
        for k, (source, target) in enumerate(((first_in, first), (second_in, second), (prior_in, prior)))
    ]
    for copy in copies:
        copy.start()
    band, columns = first.shape
    strip = SUBLANES
    tall, taller, per = strip_rows(strip)
    tiles = columns // LANES

    def windows(source, offset, reach, height):
        for block in range(band // strip):
            for tile in range(tiles):
                lanes = slice(tile * LANES, (tile + 1) * LANES)
                at = (block * tiles + tile) * per + offset
                low = block * strip - reach
                start, stop = max(low, 0), min(low + height, band)
                if start > low:
                    out[at : at + start - low, :] = jnp.zeros((start - low, LANES), jnp.float32)
                out[at + start - low : at + stop - low, :] = source[start:stop, lanes]
                if stop < low + height:
                    out[at + stop - low : at + height, :] = jnp.zeros((low + height - stop, LANES), jnp.float32)

    copies[0].wait()
    windows(first, 0, RADIUS, tall)
    copies[1].wait()
    windows(second, tall, SEARCH + RADIUS, taller)
    copies[2].wait()
    for component in range(2):
        windows(prior.at[component], tall + taller + component * strip, 0, strip)


def patch_kernel(other_first, other_second, packed, out, edge, departures):
    band, columns = other_first.shape
    strip = SUBLANES
    tall, taller, per = strip_rows(strip)
    tiles = columns // LANES
    blocks = band // strip
    here = lax.axis_index("rows")
    size = tiles * per
    last = blocks - 1
    rows_of = lambda block: pl.ds(pl.multiple_of(block * size, strip), size)
    copies = [
        pltpu.make_async_copy(
            packed.at[pl.ds(size, (blocks - 2) * size)], out.at[pl.ds(size, (blocks - 2) * size)], departures.at[0]
        ),
        pltpu.make_async_copy(packed.at[rows_of(here * last)], out.at[rows_of(here * last)], departures.at[1]),
    ]
    for copy in copies:
        copy.start()
    edge[...] = packed[rows_of((1 - here) * last), :]
    for tile in range(tiles):
        lanes = slice(tile * LANES, (tile + 1) * LANES)
        at = tile * per

        @pl.when(here > 0)
        def _():
            edge[at : at + RADIUS, :] = other_first[band - RADIUS :, lanes]
            edge[at + tall : at + tall + strip, :] = other_second[band - strip :, lanes]

        @pl.when(here == 0)
        def _():
            edge[at + tall - RADIUS : at + tall, :] = other_first[:RADIUS, lanes]
            edge[at + tall + taller - strip : at + tall + taller, :] = other_second[:strip, lanes]

    copies.append(pltpu.make_async_copy(edge, out.at[rows_of((1 - here) * last)], departures.at[2]))
    copies[2].start()
    for copy in copies:
        copy.wait()


def window_sums(rows):
    count = len(rows)
    twos = [rows[a] + rows[a + 1] for a in range(count - 1)]
    fours = [twos[a] + twos[a + 2] for a in range(count - 3)]
    eights = [fours[a] + fours[a + 4] for a in range(count - 7)]
    return [eights[a] + rows[a + 8] for a in range(count - 8)]


def split_rows(upper, lower):
    value = jnp.concatenate((upper, lower), axis=0)
    high = value.astype(jnp.bfloat16)
    rest = value - high.astype(jnp.float32)
    mid = rest.astype(jnp.bfloat16)
    low = (rest - mid.astype(jnp.float32)).astype(jnp.bfloat16)
    return high, mid, low


def lane_shift(tiles, edge, shift, lane):
    if shift > 0:
        tiles = [jnp.where(lane < shift, after, own) for own, after in zip(tiles, tiles[1:] + [edge])]
    elif shift < 0:
        tiles = [jnp.where(lane >= LANES + shift, before, own) for own, before in zip(tiles, [edge] + tiles[:-1])]
    else:
        return tiles
    return [pltpu.roll(tile, (-shift) % LANES, 1) for tile in tiles]


def plan_kernel(offsets, pair_epochs, pair_slot, inverse, lengths, table):
    count = pair_slot.shape[0]
    total = 2 * count
    cells = SPAN * SPAN

    ends = [pair_epochs[pair_slot[j], 0] for j in range(count)]
    ends += [pair_epochs[pair_slot[j], 1] for j in range(count)]
    ranks = [jnp.int32(0)] * total
    for a in range(total):
        for b in range(a + 1, total):
            ahead = (ends[a] <= ends[b]).astype(jnp.int32)
            ranks[b] = ranks[b] + ahead
            ranks[a] = ranks[a] + (1 - ahead)
    for a in range(total):
        table[a] = ranks[a]
        table[total + ranks[a]] = a
        table[2 * total + ranks[a]] = ends[a]
    for s in range(total - 1):
        width = (table[2 * total + s + 1] - table[2 * total + s]).astype(jnp.float32)
        lengths[s] = jnp.full((SUBLANES, LANES), width)

    gram = [[None] * count for _ in range(count)]
    for a in range(count):
        for b in range(a, count):
            shared = jnp.minimum(ends[count + a], ends[count + b]) - jnp.maximum(ends[a], ends[b])
            value = jnp.maximum(shared, 0).astype(jnp.float32) + (PENALTY if a == b else 0.0)
            gram[a][b] = gram[b][a] = jnp.full((SUBLANES, LANES), value)
    for k in range(count):
        pivot = 1.0 / gram[k][k]
        scaled = [gram[k][b] * pivot for b in range(count)]
        for a in range(count):
            if a == k:
                continue
            factor = gram[a][k]
            for b in range(count):
                if b != k:
                    gram[a][b] = gram[a][b] - factor * scaled[b]
            gram[a][k] = -(factor * pivot)
        for b in range(count):
            gram[k][b] = scaled[b]
        gram[k][k] = pivot
    for a in range(count):
        for b in range(count):
            inverse[a * count + b] = gram[a][b]

    first = 3 * total
    listed = first + cells - offsets.shape[0]

    def blank(cell, carry):
        table[listed + cell] = 0
        return carry

    lax.fori_loop(0, cells, blank, 0, unroll=9)

    def mark(k, carry):
        cell = (offsets[k, 1] + SEARCH) * SPAN + offsets[k, 0] + SEARCH
        table[listed + cell] = 1
        return carry

    lax.fori_loop(0, offsets.shape[0], mark, 0, unroll=8)

    def collect(cell, place):
        held = table[listed + cell]

        @pl.when(held == 0)
        def _():
            table[first + place] = cell

        return place + 1 - held

    lax.fori_loop(0, cells, collect, 0, unroll=3)


def prefix(lengths, values, running):
    total = jnp.zeros((SUBLANES, LANES), jnp.float32)
    running[0] = total
    for s, value in enumerate(values):
        total = total + lengths[s] * value
        running[s + 1] = total


def invert(count, group, fresh, observed, inverse, lengths, plan, sparse, spread, running, steps):
    segments = 2 * count - 1
    threshold = SPARSITY / PENALTY
    residual = [observed[pl.ds(group * SUBLANES * SUBLANES + j, SUBLANES, stride=SUBLANES), :] for j in range(count)]
    if not fresh:
        prefix(lengths, [spread[s] for s in range(segments)], running)
        residual = [
            residual[j] - (running[plan[count + j]] - running[plan[j]]) for j in range(count)
        ]
    for a in range(count):
        step = inverse[a * count] * residual[0]
        for b in range(1, count):
            step = step + inverse[a * count + b] * residual[b]
        steps[a] = step
        steps[count + a] = -step
    level = None
    for s in range(segments):
        rise = steps[plan[2 * count + s]]
        level = rise if level is None else level + rise
        blended = level if fresh else sparse[s + 1] + level
        scaled = jnp.clip(blended, -threshold, threshold)
        shrunk = blended - scaled
        sparse[s + 1] = shrunk
        spread[s] = shrunk - scaled


def invert_round(count, fresh, observed, inverse, lengths, plan, sparse, spread, running, steps):
    groups = len(running)

    def iterate(first):
        for group in range(groups):
            invert(
                count,
                group,
                first,
                observed,
                inverse,
                lengths,
                plan,
                sparse.at[group],
                spread.at[group],
                running[group],
                steps[group],
            )

    if fresh:
        iterate(True)

    def later(iteration, carry):
        iterate(False)
        return carry

    lax.fori_loop(1 if fresh else 0, ITERS, later, 0)


def velocity_kernel(matched, sparse_in, spread_in, inverse, lengths, plan, velocity, sparse, spread, *buffers):
    groups, held = sparse_in.shape[:2]
    segments = held - 2
    count = (segments + 1) // 2
    halves = groups // 2
    running, steps = buffers[:groups], buffers[groups:]
    bounds = 4 * count
    for group in range(groups):
        sparse[group] = sparse_in[group]
        spread[group] = spread_in[group]
    invert_round(count, False, matched, inverse, lengths, plan, sparse, spread, running, steps)

    def fill(low, high, s):
        values = [sparse[group, s] for group in range(groups)]

        def one(epoch, carry):
            for group in range(groups):
                half = group % halves
                velocity[group // halves, epoch, half * SUBLANES : (half + 1) * SUBLANES, :] = values[group]
            return carry

        lax.fori_loop(low, high, one, 0)

    fill(0, plan[bounds], 0)
    for s in range(segments):
        fill(plan[bounds + s], plan[bounds + s + 1], s + 1)
    fill(plan[bounds + segments], velocity.shape[1], segments + 1)


def signed_sums(terms):
    total = terms[SEARCH]
    moment = step = None
    for distance in range(SEARCH, 0, -1):
        below, above = terms[SEARCH - distance], terms[SEARCH + distance]
        total = total + (above + below)
        rise = above - below
        step = rise if step is None else step + rise
        moment = step if moment is None else moment + step
    return total, moment


def match(cells, first_guess, prior, predicted, table, matched):
    def pixel_tile(cell, carry):
        factors = []
        for component in range(2):
            value = prior[component * cells + cell]
            if not first_guess:
                at = pl.multiple_of((component * cells + cell) * SUBLANES, SUBLANES)
                value = 0.5 * (value + predicted[pl.ds(at, SUBLANES), :])
            nearest = jnp.clip(jnp.round(value), -float(SEARCH), float(SEARCH))
            peak = nearest * value - 0.5 * nearest * nearest
            factors.append(
                [
                    jnp.exp(value * float(shift) - (peak + 0.5 * shift * shift))
                    for shift in range(-SEARCH, SEARCH + 1)
                ]
            )
        weights, moments = [], []
        for column_shift in range(SPAN):
            total, moment = signed_sums(
                [
                    factors[0][row_shift] * table[(column_shift * SPAN + row_shift) * cells + cell]
                    for row_shift in range(SPAN)
                ]
            )
            weights.append(total * factors[1][column_shift])
            moments.append(moment * factors[1][column_shift])
        weight, column_moment = signed_sums(weights)
        row_moment = moments[0]
        for moment in moments[1:]:
            row_moment = row_moment + moment
        share = 1.0 / weight
        for component, value in enumerate((row_moment, column_moment)):
            at = pl.multiple_of((component * cells + cell) * SUBLANES, SUBLANES)
            matched[pl.ds(at, SUBLANES), :] = value * share
        return carry

    lax.fori_loop(0, cells, pixel_tile, 0)


def track_kernel(
    offsets,
    data,
    inverse,
    lengths,
    plan,
    motion,
    matched,
    sparse,
    spread,
    band,
    first,
    second,
    mean_first,
    scale_first,
    mean_second,
    scale_second,
    table,
    prior,
    predicted,
    *buffers,
):
    strip = SUBLANES
    margin = SEARCH + RADIUS
    tall = strip + 2 * RADIUS
    taller = strip + 2 * margin
    per = tall + taller + 2 * strip
    wide = strip + 2 * SEARCH
    area = float(WINDOW * WINDOW)
    count = motion.shape[0]
    columns = band.shape[1]
    tiles = columns // LANES
    cells = strip * tiles
    groups = sparse.shape[0]
    segments = 2 * count - 1
    running, steps = buffers[:groups], buffers[groups:]
    nothing = jnp.zeros((SUBLANES, LANES), jnp.float32)
    lane = lax.broadcasted_iota(jnp.int32, (SUBLANES, LANES), 1)

    tap = lax.broadcasted_iota(jnp.int32, band.shape[1:], 0)
    column = lax.broadcasted_iota(jnp.int32, band.shape[1:], 1)
    outside = jnp.where(column < LANES // 2, column + columns, column - LANES)
    for place, centre in enumerate((column, jnp.where(column < LANES, outside, -columns))):
        band[place] = jnp.where(jnp.abs(tap - centre) <= RADIUS, 1.0, 0.0).astype(jnp.bfloat16)

    def fetch(row, tile):
        return data[pl.ds(tile * per + row, SUBLANES, stride=tiles * per), :]

    for component in range(2):
        for row in range(strip):
            for tile in range(tiles):
                prior[component * cells + row * tiles + tile] = fetch(tall + taller + component * strip + row, tile)

    images = [[fetch(row, tile) for row in range(tall)] for tile in range(tiles)]
    for tile in range(tiles):
        for row in range(tall):
            first[row * tiles + tile] = images[tile][row]
    chosen = [[fetch(tall + row, tile) for row in range(taller)] for tile in range(tiles)]

    def multiply(columns_of_sums, totals, loads):
        pieces = [[], [], []]
        for sums in columns_of_sums:
            split = [split_rows(sums[row], sums[row + 1]) for row in range(0, len(sums), 2)]
            for part in range(3):
                pieces[part].append(jnp.concatenate([parts[part] for parts in split], axis=0))
        for part in range(3):
            left = jnp.concatenate(pieces[part], axis=1)
            for total, load in zip(totals, loads):
                pltpu.matmul_acc_lhs(total, left, load_staged_rhs=load if part == 0 else None)

    def statistics(*totals):
        pltpu.matmul_push_rhs(band[0], 0, 0)
        pltpu.matmul_push_rhs(band[1], 0, 1)
        square = lambda field: [[row * row for row in rows] for rows in field]
        sums_of = lambda field: [window_sums(rows) for rows in field]
        for at, field in enumerate((images, square(images))):
            multiply(sums_of(field), totals[at : at + 1], (0 if at == 0 else None,))
        for at, field in enumerate((chosen, square(chosen))):
            multiply(
                sums_of(field), (totals[2 + at], totals[4 + at]), (None, 0 if at == 0 else None)
            )
        for row in range(taller):
            pieces = [chosen[tile][row] for tile in range(tiles)]
            for shift in range(-SEARCH, SEARCH + 1):
                moved = lane_shift(pieces, nothing, shift, lane)
                for tile in range(tiles):
                    second[((shift + SEARCH) * taller + row) * tiles + tile] = moved[tile]
        totals = [pltpu.matmul_pop(total) for total in totals]
        for row in range(strip):
            for tile in range(tiles):
                at = (slice(row * SUBLANES, (row + 1) * SUBLANES), slice(tile * LANES, (tile + 1) * LANES))
                mean = totals[0][at] / area
                variance = totals[1][at] / area - mean * mean
                mean_first[row * tiles + tile] = totals[0][at]
                scale_first[row * tiles + tile] = lax.rsqrt(
                    jnp.maximum(variance, VARIANCE_FLOOR)
                ) * (SCALE / area)
        for row in range(wide):
            means, scales = [], []
            rows = slice(row * SUBLANES, (row + 1) * SUBLANES)
            for tile in range(tiles + 1):
                source = 2 if tile < tiles else 4
                lanes = slice(tile % tiles * LANES, (tile % tiles + 1) * LANES)
                mean = totals[source][rows, lanes] / area
                variance = totals[source + 1][rows, lanes] / area - mean * mean
                means.append(mean)
                scales.append(lax.rsqrt(jnp.maximum(variance, VARIANCE_FLOOR)))
            for shift in range(-SEARCH, SEARCH + 1):
                for values, held in ((means, mean_second), (scales, scale_second)):
                    moved = lane_shift(values[:tiles], values[tiles], shift, lane)
                    for tile in range(tiles):
                        held[((shift + SEARCH) * wide + row) * tiles + tile] = moved[tile]

    pl.run_scoped(
        statistics,
        *[
            pltpu.ACC(unit)((rows * SUBLANES, columns), jnp.float32)
            for unit, rows in ((0, strip), (0, strip), (0, wide), (0, wide), (1, wide), (1, wide))
        ],
    )

    def clear(index, carry):
        at = plan[6 * count + index] * cells
        for cell in range(cells):
            table[at + cell] = nothing
        return carry

    lax.fori_loop(0, SPAN * SPAN - offsets.shape[0], clear, 0)

    def place(k):
        return offsets[k, 0] + SEARCH, offsets[k, 1] + SEARCH

    def send(k, total, load):
        row_shift, column_shift = place(k)
        at_second = (column_shift * taller + row_shift) * tiles
        fields = []
        for tile in range(tiles):
            fields.append(
                window_sums(
                    [first[row * tiles + tile] * second[at_second + row * tiles + tile] for row in range(tall)]
                )
            )
        multiply(fields, (total,), (load,))

    def receive(k, total):
        row_shift, column_shift = place(k)
        at_second = (column_shift * wide + row_shift) * tiles
        at_table = (column_shift * SPAN + row_shift) * cells
        crossed = pltpu.matmul_pop(total)
        for row in range(strip):
            for tile in range(tiles):
                cell = row * tiles + tile
                value = crossed[row * SUBLANES : (row + 1) * SUBLANES, tile * LANES : (tile + 1) * LANES]
                covariance = value - mean_first[cell] * mean_second[at_second + cell]
                scaled = covariance * (scale_first[cell] * scale_second[at_second + cell])
                table[at_table + cell] = jnp.exp2(scaled)

    def all_offsets(*totals):
        pltpu.matmul_push_rhs(band[0], 0, 1)
        for member in range(GROUP):
            send(member, totals[member], 0 if member == 1 else None)

        def offset_group(group, carry):
            for member in range(GROUP):
                receive((group - 1) * GROUP + member, totals[member])
                send(group * GROUP + member, totals[member], None)
            return carry

        lax.fori_loop(1, offsets.shape[0] // GROUP, offset_group, 0)
        for member in range(GROUP):
            receive(offsets.shape[0] - GROUP + member, totals[member])

    pl.run_scoped(
        all_offsets,
        *[pltpu.ACC(member % 2)((strip * SUBLANES, columns), jnp.float32) for member in range(GROUP)],
    )

    for group in range(groups):
        sparse[group, 0] = nothing
        sparse[group, segments + 1] = nothing
    match(cells, True, prior, predicted, table, matched)
    for round_number in range(1, ROUNDS):
        invert_round(
            count, round_number == 1, matched, inverse, lengths, plan, sparse, spread, running, steps
        )
        for group in range(groups):
            prefix(lengths, [sparse[group, s + 1] for s in range(segments)], running[group])
            for j in range(count):
                predicted[pl.ds(group * SUBLANES * SUBLANES + j, SUBLANES, stride=SUBLANES), :] = (
                    running[group][plan[count + j]] - running[group][plan[j]]
                )
        match(cells, False, prior, predicted, table, matched)

    for j in range(count):
        for component in range(2):
            for tile in range(tiles):
                at = (component * cells + tile) * SUBLANES + j
                motion[j, component, :, tile * LANES : (tile + 1) * LANES] = matched[
                    pl.ds(at, SUBLANES, stride=tiles * SUBLANES), :
                ]


def by_strips(first_image, second_image, prior_motion, offsets, pair_epochs, pair_slot):
    band_rows, columns = first_image.shape[1:]
    margin = SEARCH + RADIUS
    count = lax.axis_size("pairs")
    strip = band_rows // count
    tiles = columns // LANES
    cells = strip * tiles
    tall = strip + 2 * RADIUS
    taller = strip + 2 * margin
    wide = strip + 2 * SEARCH
    per = tall + taller + 2 * strip
    vmem_spec = pl.BlockSpec(memory_space=pltpu.VMEM)
    images = (first_image[0], second_image[0])
    others = [lax.ppermute(image, "rows", [(0, 1), (1, 0)]) for image in images]
    message = (count * tiles * per, LANES)
    sources = [pltpu.with_memory_space_constraint(x, pltpu.HBM) for x in (*images, prior_motion[:, 0])]
    packed = pl.pallas_call(
        pack_kernel,
        out_shape=pltpu.VMEM(message, jnp.float32),
        in_specs=[pl.BlockSpec(memory_space=pltpu.HBM)] * 3,
        out_specs=vmem_spec,
        scratch_shapes=[pltpu.VMEM(x.shape, jnp.float32) for x in sources] + [pltpu.SemaphoreType.DMA((3,))],
        compiler_params=pltpu.CompilerParams(vmem_limit_bytes=4 * 1024 * 1024),
    )(*sources)
    packed = pl.pallas_call(
        patch_kernel,
        out_shape=pltpu.HBM(message, jnp.float32),
        in_specs=[vmem_spec] * 3,
        out_specs=pl.BlockSpec(memory_space=pltpu.HBM),
        scratch_shapes=[
            pltpu.VMEM((tiles * per, LANES), jnp.float32),
            pltpu.SemaphoreType.DMA((3,)),
        ],
        compiler_params=pltpu.CompilerParams(vmem_limit_bytes=4 * 1024 * 1024),
    )(*others, packed)
    arrived = lax.all_to_all(packed, "pairs", split_axis=0, concat_axis=0, tiled=True)
    tile = lambda *lead: pltpu.VMEM((*lead, SUBLANES, LANES), jnp.float32)
    shape = lambda *lead: jax.ShapeDtypeStruct((*lead, SUBLANES, LANES), jnp.float32)
    flat = jax.ShapeDtypeStruct((2 * cells * SUBLANES, LANES), jnp.float32)
    groups = 2 * cells // SUBLANES
    segments = 2 * count - 1
    smem = pl.BlockSpec(memory_space=pltpu.SMEM)
    vmem = pl.BlockSpec(memory_space=pltpu.VMEM)
    buffers = [tile(2 * count)] * groups + [tile(2 * count)] * groups
    entries = 6 * count + 2 * SPAN * SPAN - offsets.shape[0]
    inverse, lengths, plan = pl.pallas_call(
        plan_kernel,
        out_shape=(
            shape(count * count),
            shape(segments),
            jax.ShapeDtypeStruct((entries,), jnp.int32),
        ),
        in_specs=[smem] * 3,
        out_specs=(vmem, vmem, smem),
        compiler_params=pltpu.CompilerParams(vmem_limit_bytes=4 * 1024 * 1024),
    )(offsets, pair_epochs, pair_slot)
    motion, matched, sparse, spread = pl.pallas_call(
        track_kernel,
        out_shape=(
            jax.ShapeDtypeStruct((count, 2, strip, columns), jnp.float32),
            flat,
            shape(groups, segments + 2),
            shape(groups, segments),
        ),
        in_specs=[smem, vmem, vmem, vmem, smem],
        out_specs=(vmem, vmem, vmem, vmem),
        scratch_shapes=[
            pltpu.VMEM((2, columns, columns), jnp.bfloat16),
            tile(tall * tiles),
            tile(SPAN * taller * tiles),
            tile(cells),
            tile(cells),
            tile(SPAN * wide * tiles),
            tile(SPAN * wide * tiles),
            tile(SPAN * SPAN * cells),
            tile(2 * cells),
            pltpu.VMEM(flat.shape, jnp.float32),
            *buffers,
        ],
        compiler_params=pltpu.CompilerParams(vmem_limit_bytes=32 * 1024 * 1024),
    )(offsets, arrived, inverse, lengths, plan)
    velocity = pl.pallas_call(
        velocity_kernel,
        out_shape=jax.ShapeDtypeStruct((2, EPOCHS, cells, LANES), jnp.float32),
        in_specs=[vmem] * 5 + [smem],
        out_specs=vmem,
        scratch_shapes=[tile(groups, segments + 2), tile(groups, segments), *buffers],
        compiler_params=pltpu.CompilerParams(vmem_limit_bytes=16 * 1024 * 1024),
    )(matched, sparse, spread, inverse, lengths, plan)
    returned = lax.all_to_all(motion, "pairs", split_axis=0, concat_axis=0, tiled=True)
    returned = jnp.moveaxis(returned, 0, 1).reshape(2, 1, band_rows, columns)
    return (velocity.reshape(2, EPOCHS, 1, strip * columns), returned)


def per_device_any(first_image, second_image, *rest):
    band_rows, columns = first_image.shape[1:]
    count = lax.axis_size("pairs")
    strips = (
        count == SUBLANES
        and band_rows == count * SUBLANES
        and columns == 2 * LANES
        and lax.axis_size("rows") == 2
        and rest[1].shape[0] % GROUP == 0
    )
    plan = by_strips if strips else per_device
    return plan(first_image, second_image, *rest)


def solution(mesh):
    placed = (
        P(("groups", "pairs"), "rows", None),
        P(("groups", "pairs"), "rows", None),
        P(None, ("groups", "pairs"), "rows", None),
        P(),
        P("groups", None),
        P("groups"),
    )
    return jax.shard_map(
        per_device_any,
        mesh=mesh,
        in_specs=placed,
        out_specs=(
            P(None, None, ("groups", "rows"), "pairs"),
            P(None, ("groups", "pairs"), "rows", None),
        ),
        check_vma=False,
    )
```

```python
import functools

import jax
import jax.numpy as jnp
from jax import lax
from jax.experimental import pallas as pl
from jax.experimental.pallas import tpu as pltpu
from jax.sharding import PartitionSpec as P

OFFSETS = 64
SEARCH = 4
RADIUS = 4
EPOCHS = 128
ITERS = 4
ROUNDS = 2


SOFTMIN_HEAT = 0.1
PRIOR_STRENGTH = 0.05
PENALTY = 4.0
SPARSITY = 0.4
VARIANCE_FLOOR = 0.05
HIGHEST = lax.Precision.HIGHEST
NEWTON_STEPS = 32


def with_halo(cells, sides, width):
    for axis, dim in sides:
        count = lax.axis_size(axis)
        ends = count - 1
        head = lax.slice_in_dim(cells, 0, width, axis=dim)
        tail = lax.slice_in_dim(cells, cells.shape[dim] - width, cells.shape[dim], axis=dim)
        cells = jnp.concatenate(
            [
                lax.ppermute(tail, axis, [(i, (i + 1) % count) for i in range(ends)]),
                cells,
                lax.ppermute(head, axis, [((i + 1) % count, i) for i in range(ends)]),
            ],
            axis=dim,
        )
    return cells


def invert_normal(normal_matrix):
    order = normal_matrix.shape[0]
    identity = jnp.eye(order, dtype=jnp.float32)
    column_bound = jnp.max(jnp.sum(jnp.abs(normal_matrix), axis=0))
    estimate = identity / column_bound
    for step in range(NEWTON_STEPS):
        product = jnp.dot(normal_matrix, estimate, precision=HIGHEST)
        estimate = jnp.dot(estimate, 2.0 * identity - product, precision=HIGHEST)
    return estimate


def box_sum(values):
    window = 2 * RADIUS + 1
    height = values.shape[-2] - 2 * RADIUS
    breadth = values.shape[-1] - 2 * RADIUS
    running = values[..., 0:height, :]
    for position in range(1, window):
        running = running + values[..., position : position + height, :]
    summed = running[..., 0:breadth]
    for position in range(1, window):
        summed = summed + running[..., position : position + breadth]
    return summed / float(window * window)


def correlate(
    shift_vector,
    first_padded,
    second_padded,
    mean_first,
    var_first,
    mean_second_all,
    square_second_all,
    height,
    columns,
):
    row_start = shift_vector[0] + SEARCH
    col_start = shift_vector[1] + SEARCH
    mean_second = lax.dynamic_slice(mean_second_all, (row_start, col_start), (height, columns))
    square_second = lax.dynamic_slice(square_second_all, (row_start, col_start), (height, columns))
    window_second = lax.dynamic_slice(
        second_padded, (row_start, col_start), (height + 2 * RADIUS, columns + 2 * RADIUS)
    )
    covariance = box_sum(first_padded * window_second) - mean_first * mean_second
    var_second = square_second - mean_second * mean_second
    return covariance / jnp.sqrt(
        jnp.maximum(var_first, VARIANCE_FLOOR) * jnp.maximum(var_second, VARIANCE_FLOOR)
    )


def build_design(pair_epochs, pair_slot):
    pair_number = jnp.arange(pair_slot.shape[0], dtype=jnp.int32)
    chooser = (pair_slot[:, None] == pair_number[None, :]).astype(jnp.int32)
    starts = jnp.sum(chooser * pair_epochs[None, :, 0], axis=1)
    finishes = jnp.sum(chooser * pair_epochs[None, :, 1], axis=1)
    epoch_number = jnp.arange(EPOCHS, dtype=jnp.int32)
    inside = (epoch_number[None, :] >= starts[:, None]) & (
        epoch_number[None, :] < finishes[:, None]
    )
    return inside.astype(jnp.float32)


def per_device(first_image, second_image, prior_motion, offsets, pair_epochs, pair_slot):
    band_rows = first_image.shape[1]
    columns = first_image.shape[2]
    margin = SEARCH + RADIUS
    stacked = jnp.concatenate((first_image, second_image), axis=0)
    extended = with_halo(stacked, (("rows", 1),), margin)
    extended = jnp.pad(extended, ((0, 0), (0, 0), (margin, margin)))
    first_padded = extended[
        0, SEARCH : SEARCH + band_rows + 2 * RADIUS, SEARCH : SEARCH + columns + 2 * RADIUS
    ]
    second_padded = extended[1]
    mean_first = box_sum(first_padded)
    var_first = box_sum(first_padded * first_padded) - mean_first * mean_first
    mean_second_all = box_sum(second_padded)
    square_second_all = box_sum(second_padded * second_padded)
    offset_blocks = offsets.reshape(OFFSETS // 8, 8, 2)
    pairs_count = lax.axis_size("pairs")
    pixels = band_rows * columns // pairs_count
    design_matrix = build_design(pair_epochs, pair_slot)
    normal_matrix = jnp.dot(design_matrix.T, design_matrix, precision=HIGHEST) + PENALTY * jnp.eye(
        EPOCHS, dtype=jnp.float32
    )
    inverse_matrix = invert_normal(normal_matrix)
    threshold = SPARSITY / PENALTY
    sparse = jnp.zeros((2, EPOCHS, pixels), jnp.float32)
    scaled = jnp.zeros((2, EPOCHS, pixels), jnp.float32)
    prior_band = prior_motion[:, 0]
    motion = prior_band
    for round_number in range(ROUNDS):

        def block_step(state_now, offset_block):
            running_max, weight_sum, sum_rows, sum_cols = state_now
            cross_correlation = jax.vmap(
                lambda shift_vector: correlate(
                    shift_vector,
                    first_padded,
                    second_padded,
                    mean_first,
                    var_first,
                    mean_second_all,
                    square_second_all,
                    band_rows,
                    columns,
                )
            )(offset_block)
            shifts = offset_block.astype(jnp.float32)
            pixel_distance = (shifts[:, 0, None, None] - prior_band[0]) ** 2 + (
                shifts[:, 1, None, None] - prior_band[1]
            ) ** 2
            match_scores = (cross_correlation - PRIOR_STRENGTH * pixel_distance) / SOFTMIN_HEAT
            new_max = jnp.maximum(running_max, jnp.max(match_scores, axis=0))
            rescale = jnp.exp(running_max - new_max)
            weights = jnp.exp(match_scores - new_max)
            weight_sum = weight_sum * rescale + jnp.sum(weights, axis=0)
            sum_rows = sum_rows * rescale + jnp.sum(weights * shifts[:, 0, None, None], axis=0)
            sum_cols = sum_cols * rescale + jnp.sum(weights * shifts[:, 1, None, None], axis=0)
            return ((new_max, weight_sum, sum_rows, sum_cols), None)

        zeros_band = jnp.zeros((band_rows, columns), jnp.float32)
        initial = (
            jnp.full((band_rows, columns), -jnp.inf, jnp.float32),
            zeros_band,
            zeros_band,
            zeros_band,
        )
        (running_max, weight_sum, sum_rows, sum_cols), unused = lax.scan(
            block_step, initial, offset_blocks
        )
        motion = jnp.stack((sum_rows / weight_sum, sum_cols / weight_sum))
        outgoing = motion.reshape(2, 1, pairs_count, pixels)
        arrived = lax.all_to_all(outgoing, "pairs", split_axis=2, concat_axis=1, tiled=True)
        observed = arrived.reshape(2, arrived.shape[1], pixels)
        fixed_part = jnp.einsum("pe,cpn->cen", design_matrix, observed, precision=HIGHEST)
        for iteration in range(ITERS):
            target = fixed_part + PENALTY * (sparse - scaled)
            estimate = jnp.einsum("ef,cfn->cen", inverse_matrix, target, precision=HIGHEST)
            blended = estimate + scaled
            sparse = blended - jnp.clip(blended, -threshold, threshold)
            scaled = blended - sparse
        if round_number + 1 < ROUNDS:
            predicted = jnp.einsum("pe,cen->cpn", design_matrix, sparse, precision=HIGHEST)
            predicted = predicted.reshape(2, predicted.shape[1], 1, pixels)
            returned = lax.all_to_all(predicted, "pairs", split_axis=1, concat_axis=2, tiled=True)
            prior_band = 0.5 * (prior_motion[:, 0] + returned.reshape(2, band_rows, columns))
    return (sparse[:, :, None, :], motion[:, None])


LANES = 128
SUBLANES = 8
GROUP = 16
SPAN = 2 * SEARCH + 1
WINDOW = 2 * RADIUS + 1
LOG2E = 1.4426950408889634
SCALE = LOG2E / SOFTMIN_HEAT


def strip_rows(strip):
    tall = strip + 2 * RADIUS
    taller = strip + 2 * (SEARCH + RADIUS)
    return tall, taller, tall + taller + 2 * strip


def pack_kernel(first_in, second_in, prior_in, out, first, second, prior, arrivals):
    copies = [
        pltpu.make_async_copy(source, target, arrivals.at[k])
        for k, (source, target) in enumerate(((first_in, first), (second_in, second), (prior_in, prior)))
    ]
    for copy in copies:
        copy.start()
    band, columns = first.shape
    strip = SUBLANES
    tall, taller, per = strip_rows(strip)
    tiles = columns // LANES

    def windows(source, offset, reach, height):
        for block in range(band // strip):
            for tile in range(tiles):
                lanes = slice(tile * LANES, (tile + 1) * LANES)
                at = (block * tiles + tile) * per + offset
                low = block * strip - reach
                start, stop = max(low, 0), min(low + height, band)
                if start > low:
                    out[at : at + start - low, :] = jnp.zeros((start - low, LANES), jnp.float32)
                out[at + start - low : at + stop - low, :] = source[start:stop, lanes]
                if stop < low + height:
                    out[at + stop - low : at + height, :] = jnp.zeros((low + height - stop, LANES), jnp.float32)

    copies[0].wait()
    windows(first, 0, RADIUS, tall)
    copies[1].wait()
    windows(second, tall, SEARCH + RADIUS, taller)
    copies[2].wait()
    for component in range(2):
        windows(prior.at[component], tall + taller + component * strip, 0, strip)


def patch_kernel(other_first, other_second, packed, out, edge, departures):
    band, columns = other_first.shape
    strip = SUBLANES
    tall, taller, per = strip_rows(strip)
    tiles = columns // LANES
    blocks = band // strip
    here = lax.axis_index("rows")
    size = tiles * per
    last = blocks - 1
    rows_of = lambda block: pl.ds(pl.multiple_of(block * size, strip), size)
    copies = [
        pltpu.make_async_copy(
            packed.at[pl.ds(size, (blocks - 2) * size)], out.at[pl.ds(size, (blocks - 2) * size)], departures.at[0]
        ),
        pltpu.make_async_copy(packed.at[rows_of(here * last)], out.at[rows_of(here * last)], departures.at[1]),
    ]
    for copy in copies:
        copy.start()
    edge[...] = packed[rows_of((1 - here) * last), :]
    for tile in range(tiles):
        lanes = slice(tile * LANES, (tile + 1) * LANES)
        at = tile * per

        @pl.when(here > 0)
        def _():
            edge[at : at + RADIUS, :] = other_first[band - RADIUS :, lanes]
            edge[at + tall : at + tall + strip, :] = other_second[band - strip :, lanes]

        @pl.when(here == 0)
        def _():
            edge[at + tall - RADIUS : at + tall, :] = other_first[:RADIUS, lanes]
            edge[at + tall + taller - strip : at + tall + taller, :] = other_second[:strip, lanes]

    copies.append(pltpu.make_async_copy(edge, out.at[rows_of((1 - here) * last)], departures.at[2]))
    copies[2].start()
    for copy in copies:
        copy.wait()


def window_sums(rows):
    sums = []
    for top in range(0, len(rows) - WINDOW + 1, WINDOW - 1):
        size = min(WINDOW - 1, len(rows) - WINDOW + 1 - top)
        before = [rows[top + WINDOW - 2]]
        for row in range(WINDOW - 3, -1, -1):
            before.append(rows[top + row] + before[-1])
        before.reverse()
        after = rows[top + WINDOW - 1]
        for row in range(size):
            sums.append(before[row] + after)
            if row + 1 < size:
                after = after + rows[top + WINDOW + row]
    return sums


def split_rows(upper, lower):
    value = jnp.concatenate((upper, lower), axis=0)
    high = value.astype(jnp.bfloat16)
    rest = value - high.astype(jnp.float32)
    mid = rest.astype(jnp.bfloat16)
    low = (rest - mid.astype(jnp.float32)).astype(jnp.bfloat16)
    return high, mid, low


def lane_shift(tiles, edge, shift, lane):
    if shift > 0:
        tiles = [jnp.where(lane < shift, after, own) for own, after in zip(tiles, tiles[1:] + [edge])]
    elif shift < 0:
        tiles = [jnp.where(lane >= LANES + shift, before, own) for own, before in zip(tiles, [edge] + tiles[:-1])]
    else:
        return tiles
    return [pltpu.roll(tile, (-shift) % LANES, 1) for tile in tiles]


def plan_kernel(offsets, pair_epochs, pair_slot, inverse, lengths, table):
    count = pair_slot.shape[0]
    total = 2 * count
    cells = SPAN * SPAN

    ends = [pair_epochs[pair_slot[j], 0] for j in range(count)]
    ends += [pair_epochs[pair_slot[j], 1] for j in range(count)]
    ranks = [jnp.int32(0)] * total
    for a in range(total):
        for b in range(a + 1, total):
            ahead = (ends[a] <= ends[b]).astype(jnp.int32)
            ranks[b] = ranks[b] + ahead
            ranks[a] = ranks[a] + (1 - ahead)
    for a in range(total):
        table[a] = ranks[a]
        table[total + ranks[a]] = a
        table[2 * total + ranks[a]] = ends[a]
    for s in range(total - 1):
        width = (table[2 * total + s + 1] - table[2 * total + s]).astype(jnp.float32)
        lengths[s] = jnp.full((SUBLANES, LANES), width)

    gram = [[None] * count for _ in range(count)]
    for a in range(count):
        for b in range(a, count):
            shared = jnp.minimum(ends[count + a], ends[count + b]) - jnp.maximum(ends[a], ends[b])
            value = jnp.maximum(shared, 0).astype(jnp.float32) + (PENALTY if a == b else 0.0)
            gram[a][b] = gram[b][a] = jnp.full((SUBLANES, LANES), value)
    for k in range(count):
        pivot = 1.0 / gram[k][k]
        scaled = [gram[k][b] * pivot for b in range(count)]
        for a in range(count):
            if a == k:
                continue
            factor = gram[a][k]
            for b in range(count):
                if b != k:
                    gram[a][b] = gram[a][b] - factor * scaled[b]
            gram[a][k] = -(factor * pivot)
        for b in range(count):
            gram[k][b] = scaled[b]
        gram[k][k] = pivot
    for a in range(count):
        for b in range(count):
            inverse[a * count + b] = gram[a][b]

    first = 3 * total
    listed = first + cells - offsets.shape[0]

    def blank(cell, carry):
        table[listed + cell] = 0
        return carry

    lax.fori_loop(0, cells, blank, 0, unroll=9)

    def mark(k, carry):
        cell = (offsets[k, 1] + SEARCH) * SPAN + offsets[k, 0] + SEARCH
        table[listed + cell] = 1
        return carry

    lax.fori_loop(0, offsets.shape[0], mark, 0, unroll=8)

    def collect(cell, place):
        held = table[listed + cell]

        @pl.when(held == 0)
        def _():
            table[first + place] = cell

        return place + 1 - held

    lax.fori_loop(0, cells, collect, 0, unroll=3)


def prefix(lengths, values, running):
    total = jnp.zeros((SUBLANES, LANES), jnp.float32)
    running[0] = total
    for s, value in enumerate(values):
        total = total + lengths[s] * value
        running[s + 1] = total


def invert(count, group, fresh, observed, inverse, lengths, plan, sparse, spread, running, steps):
    segments = 2 * count - 1
    threshold = SPARSITY / PENALTY
    residual = [observed[pl.ds(group * SUBLANES * SUBLANES + j, SUBLANES, stride=SUBLANES), :] for j in range(count)]
    if not fresh:
        prefix(lengths, [spread[s] for s in range(segments)], running)
        residual = [
            residual[j] - (running[plan[count + j]] - running[plan[j]]) for j in range(count)
        ]
    for a in range(count):
        step = inverse[a * count] * residual[0]
        for b in range(1, count):
            step = step + inverse[a * count + b] * residual[b]
        steps[a] = step
        steps[count + a] = -step
    level = None
    for s in range(segments):
        rise = steps[plan[2 * count + s]]
        level = rise if level is None else level + rise
        blended = level if fresh else sparse[s + 1] + level
        scaled = jnp.clip(blended, -threshold, threshold)
        shrunk = blended - scaled
        sparse[s + 1] = shrunk
        spread[s] = shrunk - scaled


def invert_round(count, fresh, observed, inverse, lengths, plan, sparse, spread, running, steps):
    groups = len(running)

    def iterate(first):
        for group in range(groups):
            invert(
                count,
                group,
                first,
                observed,
                inverse,
                lengths,
                plan,
                sparse.at[group],
                spread.at[group],
                running[group],
                steps[group],
            )

    if fresh:
        iterate(True)

    def later(iteration, carry):
        iterate(False)
        return carry

    lax.fori_loop(1 if fresh else 0, ITERS, later, 0, unroll=True)


def velocity_kernel(matched, sparse_in, spread_in, inverse, lengths, plan, velocity, sparse, spread, *buffers):
    groups, held = sparse_in.shape[:2]
    segments = held - 2
    count = (segments + 1) // 2
    halves = groups // 2
    running, steps = buffers[:groups], buffers[groups:]
    bounds = 4 * count
    for group in range(groups):
        sparse[group] = sparse_in[group]
        spread[group] = spread_in[group]
    invert_round(count, False, matched, inverse, lengths, plan, sparse, spread, running, steps)

    def fill(low, high, s):
        values = [sparse[group, s] for group in range(groups)]

        def one(epoch, carry):
            for group in range(groups):
                half = group % halves
                velocity[group // halves, epoch, half * SUBLANES : (half + 1) * SUBLANES, :] = values[group]
            return carry

        lax.fori_loop(low, high, one, 0)

    fill(0, plan[bounds], 0)
    for s in range(segments):
        fill(plan[bounds + s], plan[bounds + s + 1], s + 1)
    fill(plan[bounds + segments], velocity.shape[1], segments + 1)


def signed_sums(terms):
    total = terms[SEARCH]
    moment = step = None
    for distance in range(SEARCH, 0, -1):
        below, above = terms[SEARCH - distance], terms[SEARCH + distance]
        total = total + (above + below)
        rise = above - below
        step = rise if step is None else step + rise
        moment = step if moment is None else moment + step
    return total, moment


def match(cells, first_guess, prior, predicted, table, matched):
    def pixel_tile(cell, carry):
        factors = []
        for component in range(2):
            value = prior[component * cells + cell]
            if not first_guess:
                at = pl.multiple_of((component * cells + cell) * SUBLANES, SUBLANES)
                value = 0.5 * (value + predicted[pl.ds(at, SUBLANES), :])
            nearest = jnp.clip(jnp.round(value), -float(SEARCH), float(SEARCH))
            centre = nearest * (0.5 * LOG2E * nearest - LOG2E * value)
            slope = LOG2E * value
            powers = {0: jnp.exp2(centre)}
            for shift in range(1, SEARCH + 1):
                level = centre - 0.5 * LOG2E * shift * shift
                rise = slope * float(shift)
                powers[shift] = jnp.exp2(level + rise)
                powers[-shift] = jnp.exp2(level - rise)
            factors.append([powers[shift] for shift in range(-SEARCH, SEARCH + 1)])
        weights, moments = [], []
        for column_shift in range(SPAN):
            total, moment = signed_sums(
                [
                    factors[0][row_shift] * table[(column_shift * SPAN + row_shift) * cells + cell]
                    for row_shift in range(SPAN)
                ]
            )
            weights.append(total * factors[1][column_shift])
            moments.append(moment * factors[1][column_shift])
        weight, column_moment = signed_sums(weights)
        row_moment = moments[0]
        for moment in moments[1:]:
            row_moment = row_moment + moment
        share = 1.0 / weight
        for component, value in enumerate((row_moment, column_moment)):
            at = pl.multiple_of((component * cells + cell) * SUBLANES, SUBLANES)
            matched[pl.ds(at, SUBLANES), :] = value * share
        return carry

    lax.fori_loop(0, cells, pixel_tile, 0, unroll=2)


def track_kernel(
    offsets,
    data,
    inverse,
    lengths,
    plan,
    motion,
    matched,
    sparse,
    spread,
    band,
    first,
    second,
    mean_first,
    scale_first,
    mean_second,
    scale_second,
    table,
    prior,
    predicted,
    *buffers,
):
    strip = SUBLANES
    margin = SEARCH + RADIUS
    tall = strip + 2 * RADIUS
    taller = strip + 2 * margin
    per = tall + taller + 2 * strip
    wide = strip + 2 * SEARCH
    area = float(WINDOW * WINDOW)
    count = motion.shape[0]
    columns = band.shape[1]
    tiles = columns // LANES
    cells = strip * tiles
    groups = sparse.shape[0]
    segments = 2 * count - 1
    running, steps = buffers[:groups], buffers[groups:]
    nothing = jnp.zeros((SUBLANES, LANES), jnp.float32)
    lane = lax.broadcasted_iota(jnp.int32, (SUBLANES, LANES), 1)

    def clear(index, carry):
        at = plan[6 * count + index] * cells
        for cell in range(cells):
            table[at + cell] = nothing
        return carry

    lax.fori_loop(0, SPAN * SPAN - offsets.shape[0], clear, 0)

    tap = lax.broadcasted_iota(jnp.int32, band.shape[1:], 0)
    column = lax.broadcasted_iota(jnp.int32, band.shape[1:], 1)
    outside = jnp.where(column < LANES // 2, column + columns, column - LANES)
    for place, centre in enumerate((column, jnp.where(column < LANES, outside, -columns))):
        band[place] = jnp.where(jnp.abs(tap - centre) <= RADIUS, 1.0, 0.0).astype(jnp.bfloat16)

    def fetch(row, tile):
        return data[pl.ds(tile * per + row, SUBLANES, stride=tiles * per), :]

    for component in range(2):
        for row in range(strip):
            for tile in range(tiles):
                prior[component * cells + row * tiles + tile] = fetch(tall + taller + component * strip + row, tile)

    images = [[fetch(row, tile) for row in range(tall)] for tile in range(tiles)]
    for tile in range(tiles):
        for row in range(tall):
            first[row * tiles + tile] = images[tile][row]
    chosen = [[fetch(tall + row, tile) for row in range(taller)] for tile in range(tiles)]

    def multiply(columns_of_sums, totals, loads):
        pieces = [[], [], []]
        for sums in columns_of_sums:
            split = [split_rows(sums[row], sums[row + 1]) for row in range(0, len(sums), 2)]
            for part in range(3):
                pieces[part].append(jnp.concatenate([parts[part] for parts in split], axis=0))
        for part in range(3):
            left = jnp.concatenate(pieces[part], axis=1)
            for total, load in zip(totals, loads):
                pltpu.matmul_acc_lhs(total, left, load_staged_rhs=load if part == 0 else None)

    def statistics(*totals):
        pltpu.matmul_push_rhs(band[0], 0, 0)
        pltpu.matmul_push_rhs(band[1], 0, 1)
        square = lambda field: [[row * row for row in rows] for rows in field]
        sums_of = lambda field: [window_sums(rows) for rows in field]
        for at, field in enumerate((images, square(images))):
            multiply(sums_of(field), totals[at : at + 1], (0 if at == 0 else None,))
        for at, field in enumerate((chosen, square(chosen))):
            multiply(
                sums_of(field), (totals[2 + at], totals[4 + at]), (None, 0 if at == 0 else None)
            )
        for row in range(taller):
            pieces = [chosen[tile][row] for tile in range(tiles)]
            for shift in range(-SEARCH, SEARCH + 1):
                moved = lane_shift(pieces, nothing, shift, lane)
                for tile in range(tiles):
                    second[((shift + SEARCH) * taller + row) * tiles + tile] = moved[tile]
        totals = [pltpu.matmul_pop(total) for total in totals]
        for row in range(strip):
            for tile in range(tiles):
                at = (slice(row * SUBLANES, (row + 1) * SUBLANES), slice(tile * LANES, (tile + 1) * LANES))
                mean = totals[0][at] / area
                variance = totals[1][at] / area - mean * mean
                mean_first[row * tiles + tile] = totals[0][at]
                scale_first[row * tiles + tile] = lax.rsqrt(
                    jnp.maximum(variance, VARIANCE_FLOOR)
                ) * (SCALE / area)
        for row in range(wide):
            means, scales = [], []
            rows = slice(row * SUBLANES, (row + 1) * SUBLANES)
            for tile in range(tiles + 1):
                source = 2 if tile < tiles else 4
                lanes = slice(tile % tiles * LANES, (tile % tiles + 1) * LANES)
                mean = totals[source][rows, lanes] / area
                variance = totals[source + 1][rows, lanes] / area - mean * mean
                means.append(mean)
                scales.append(lax.rsqrt(jnp.maximum(variance, VARIANCE_FLOOR)))
            for shift in range(-SEARCH, SEARCH + 1):
                for values, held in ((means, mean_second), (scales, scale_second)):
                    moved = lane_shift(values[:tiles], values[tiles], shift, lane)
                    for tile in range(tiles):
                        held[((shift + SEARCH) * wide + row) * tiles + tile] = moved[tile]

    pl.run_scoped(
        statistics,
        *[
            pltpu.ACC(unit)((rows * SUBLANES, columns), jnp.float32)
            for unit, rows in ((0, strip), (0, strip), (0, wide), (0, wide), (1, wide), (1, wide))
        ],
    )

    def place(k):
        return offsets[k, 0] + SEARCH, offsets[k, 1] + SEARCH

    def send(k, total, load):
        row_shift, column_shift = place(k)
        at_second = (column_shift * taller + row_shift) * tiles
        fields = []
        for tile in range(tiles):
            fields.append(
                window_sums(
                    [first[row * tiles + tile] * second[at_second + row * tiles + tile] for row in range(tall)]
                )
            )
        multiply(fields, (total,), (load,))

    def receive(k, total):
        row_shift, column_shift = place(k)
        at_second = (column_shift * wide + row_shift) * tiles
        at_table = (column_shift * SPAN + row_shift) * cells
        crossed = pltpu.matmul_pop(total)
        for row in range(strip):
            for tile in range(tiles):
                cell = row * tiles + tile
                value = crossed[row * SUBLANES : (row + 1) * SUBLANES, tile * LANES : (tile + 1) * LANES]
                covariance = value - mean_first[cell] * mean_second[at_second + cell]
                scaled = covariance * (scale_first[cell] * scale_second[at_second + cell])
                table[at_table + cell] = jnp.exp2(scaled)

    def all_offsets(*totals):
        pltpu.matmul_push_rhs(band[0], 0, 1)
        for member in range(GROUP):
            send(member, totals[member], 0 if member == 1 else None)

        def offset_group(group, carry):
            for member in range(GROUP):
                receive((group - 1) * GROUP + member, totals[member])
                send(group * GROUP + member, totals[member], None)
            return carry

        lax.fori_loop(1, offsets.shape[0] // GROUP, offset_group, 0)
        for member in range(GROUP):
            receive(offsets.shape[0] - GROUP + member, totals[member])

    pl.run_scoped(
        all_offsets,
        *[pltpu.ACC(member % 2)((strip * SUBLANES, columns), jnp.float32) for member in range(GROUP)],
    )

    for group in range(groups):
        sparse[group, 0] = nothing
        sparse[group, segments + 1] = nothing
    match(cells, True, prior, predicted, table, matched)
    for round_number in range(1, ROUNDS):
        invert_round(
            count, round_number == 1, matched, inverse, lengths, plan, sparse, spread, running, steps
        )
        for group in range(groups):
            prefix(lengths, [sparse[group, s + 1] for s in range(segments)], running[group])
            for j in range(count):
                predicted[pl.ds(group * SUBLANES * SUBLANES + j, SUBLANES, stride=SUBLANES), :] = (
                    running[group][plan[count + j]] - running[group][plan[j]]
                )
        match(cells, False, prior, predicted, table, matched)

    for j in range(count):
        for component in range(2):
            for tile in range(tiles):
                at = (component * cells + tile) * SUBLANES + j
                motion[j, component, :, tile * LANES : (tile + 1) * LANES] = matched[
                    pl.ds(at, SUBLANES, stride=tiles * SUBLANES), :
                ]


def by_strips(first_image, second_image, prior_motion, offsets, pair_epochs, pair_slot):
    band_rows, columns = first_image.shape[1:]
    margin = SEARCH + RADIUS
    count = lax.axis_size("pairs")
    strip = band_rows // count
    tiles = columns // LANES
    cells = strip * tiles
    tall = strip + 2 * RADIUS
    taller = strip + 2 * margin
    wide = strip + 2 * SEARCH
    per = tall + taller + 2 * strip
    vmem_spec = pl.BlockSpec(memory_space=pltpu.VMEM)
    images = (first_image[0], second_image[0])
    others = [lax.ppermute(image, "rows", [(0, 1), (1, 0)]) for image in images]
    message = (count * tiles * per, LANES)
    sources = [pltpu.with_memory_space_constraint(x, pltpu.HBM) for x in (*images, prior_motion[:, 0])]
    packed = pl.pallas_call(
        pack_kernel,
        out_shape=pltpu.VMEM(message, jnp.float32),
        in_specs=[pl.BlockSpec(memory_space=pltpu.HBM)] * 3,
        out_specs=vmem_spec,
        scratch_shapes=[pltpu.VMEM(x.shape, jnp.float32) for x in sources] + [pltpu.SemaphoreType.DMA((3,))],
        compiler_params=pltpu.CompilerParams(vmem_limit_bytes=4 * 1024 * 1024),
    )(*sources)
    packed = pl.pallas_call(
        patch_kernel,
        out_shape=pltpu.HBM(message, jnp.float32),
        in_specs=[vmem_spec] * 3,
        out_specs=pl.BlockSpec(memory_space=pltpu.HBM),
        scratch_shapes=[
            pltpu.VMEM((tiles * per, LANES), jnp.float32),
            pltpu.SemaphoreType.DMA((3,)),
        ],
        compiler_params=pltpu.CompilerParams(vmem_limit_bytes=4 * 1024 * 1024),
    )(*others, packed)
    arrived = lax.all_to_all(packed, "pairs", split_axis=0, concat_axis=0, tiled=True)
    tile = lambda *lead: pltpu.VMEM((*lead, SUBLANES, LANES), jnp.float32)
    shape = lambda *lead: jax.ShapeDtypeStruct((*lead, SUBLANES, LANES), jnp.float32)
    flat = jax.ShapeDtypeStruct((2 * cells * SUBLANES, LANES), jnp.float32)
    groups = 2 * cells // SUBLANES
    segments = 2 * count - 1
    smem = pl.BlockSpec(memory_space=pltpu.SMEM)
    vmem = pl.BlockSpec(memory_space=pltpu.VMEM)
    buffers = [tile(2 * count)] * groups + [tile(2 * count)] * groups
    entries = 6 * count + 2 * SPAN * SPAN - offsets.shape[0]
    inverse, lengths, plan = pl.pallas_call(
        plan_kernel,
        out_shape=(
            shape(count * count),
            shape(segments),
            jax.ShapeDtypeStruct((entries,), jnp.int32),
        ),
        in_specs=[smem] * 3,
        out_specs=(vmem, vmem, smem),
        compiler_params=pltpu.CompilerParams(vmem_limit_bytes=4 * 1024 * 1024),
    )(offsets, pair_epochs, pair_slot)
    motion, matched, sparse, spread = pl.pallas_call(
        track_kernel,
        out_shape=(
            jax.ShapeDtypeStruct((count, 2, strip, columns), jnp.float32),
            flat,
            shape(groups, segments + 2),
            shape(groups, segments),
        ),
        in_specs=[smem, vmem, vmem, vmem, smem],
        out_specs=(vmem, vmem, vmem, vmem),
        scratch_shapes=[
            pltpu.VMEM((2, columns, columns), jnp.bfloat16),
            tile(tall * tiles),
            tile(SPAN * taller * tiles),
            tile(cells),
            tile(cells),
            tile(SPAN * wide * tiles),
            tile(SPAN * wide * tiles),
            tile(SPAN * SPAN * cells),
            tile(2 * cells),
            pltpu.VMEM(flat.shape, jnp.float32),
            *buffers,
        ],
        compiler_params=pltpu.CompilerParams(vmem_limit_bytes=32 * 1024 * 1024),
    )(offsets, arrived, inverse, lengths, plan)
    velocity = pl.pallas_call(
        velocity_kernel,
        out_shape=jax.ShapeDtypeStruct((2, EPOCHS, cells, LANES), jnp.float32),
        in_specs=[vmem] * 5 + [smem],
        out_specs=vmem,
        scratch_shapes=[tile(groups, segments + 2), tile(groups, segments), *buffers],
        compiler_params=pltpu.CompilerParams(vmem_limit_bytes=16 * 1024 * 1024),
    )(matched, sparse, spread, inverse, lengths, plan)
    returned = lax.all_to_all(motion, "pairs", split_axis=0, concat_axis=0, tiled=True)
    returned = jnp.moveaxis(returned, 0, 1).reshape(2, 1, band_rows, columns)
    return (velocity.reshape(2, EPOCHS, 1, strip * columns), returned)


def per_device_any(first_image, second_image, *rest):
    band_rows, columns = first_image.shape[1:]
    count = lax.axis_size("pairs")
    strips = (
        count == SUBLANES
        and band_rows == count * SUBLANES
        and columns == 2 * LANES
        and lax.axis_size("rows") == 2
        and rest[1].shape[0] % GROUP == 0
    )
    plan = by_strips if strips else per_device
    return plan(first_image, second_image, *rest)


def solution(mesh):
    placed = (
        P(("groups", "pairs"), "rows", None),
        P(("groups", "pairs"), "rows", None),
        P(None, ("groups", "pairs"), "rows", None),
        P(),
        P("groups", None),
        P("groups"),
    )
    return jax.shard_map(
        per_device_any,
        mesh=mesh,
        in_specs=placed,
        out_specs=(
            P(None, None, ("groups", "rows"), "pairs"),
            P(None, ("groups", "pairs"), "rows", None),
        ),
        check_vma=False,
    )
```

```python
import functools

import jax
import jax.numpy as jnp
from jax import lax
from jax.experimental import pallas as pl
from jax.experimental.pallas import tpu as pltpu
from jax.sharding import PartitionSpec as P

OFFSETS = 64
SEARCH = 4
RADIUS = 4
EPOCHS = 128
ITERS = 4
ROUNDS = 2


SOFTMIN_HEAT = 0.1
PRIOR_STRENGTH = 0.05
PENALTY = 4.0
SPARSITY = 0.4
VARIANCE_FLOOR = 0.05
HIGHEST = lax.Precision.HIGHEST
NEWTON_STEPS = 32


def with_halo(cells, sides, width):
    for axis, dim in sides:
        count = lax.axis_size(axis)
        ends = count - 1
        head = lax.slice_in_dim(cells, 0, width, axis=dim)
        tail = lax.slice_in_dim(cells, cells.shape[dim] - width, cells.shape[dim], axis=dim)
        cells = jnp.concatenate(
            [
                lax.ppermute(tail, axis, [(i, (i + 1) % count) for i in range(ends)]),
                cells,
                lax.ppermute(head, axis, [((i + 1) % count, i) for i in range(ends)]),
            ],
            axis=dim,
        )
    return cells


def invert_normal(normal_matrix):
    order = normal_matrix.shape[0]
    identity = jnp.eye(order, dtype=jnp.float32)
    column_bound = jnp.max(jnp.sum(jnp.abs(normal_matrix), axis=0))
    estimate = identity / column_bound
    for step in range(NEWTON_STEPS):
        product = jnp.dot(normal_matrix, estimate, precision=HIGHEST)
        estimate = jnp.dot(estimate, 2.0 * identity - product, precision=HIGHEST)
    return estimate


def box_sum(values):
    window = 2 * RADIUS + 1
    height = values.shape[-2] - 2 * RADIUS
    breadth = values.shape[-1] - 2 * RADIUS
    running = values[..., 0:height, :]
    for position in range(1, window):
        running = running + values[..., position : position + height, :]
    summed = running[..., 0:breadth]
    for position in range(1, window):
        summed = summed + running[..., position : position + breadth]
    return summed / float(window * window)


def correlate(
    shift_vector,
    first_padded,
    second_padded,
    mean_first,
    var_first,
    mean_second_all,
    square_second_all,
    height,
    columns,
):
    row_start = shift_vector[0] + SEARCH
    col_start = shift_vector[1] + SEARCH
    mean_second = lax.dynamic_slice(mean_second_all, (row_start, col_start), (height, columns))
    square_second = lax.dynamic_slice(square_second_all, (row_start, col_start), (height, columns))
    window_second = lax.dynamic_slice(
        second_padded, (row_start, col_start), (height + 2 * RADIUS, columns + 2 * RADIUS)
    )
    covariance = box_sum(first_padded * window_second) - mean_first * mean_second
    var_second = square_second - mean_second * mean_second
    return covariance / jnp.sqrt(
        jnp.maximum(var_first, VARIANCE_FLOOR) * jnp.maximum(var_second, VARIANCE_FLOOR)
    )


def build_design(pair_epochs, pair_slot):
    pair_number = jnp.arange(pair_slot.shape[0], dtype=jnp.int32)
    chooser = (pair_slot[:, None] == pair_number[None, :]).astype(jnp.int32)
    starts = jnp.sum(chooser * pair_epochs[None, :, 0], axis=1)
    finishes = jnp.sum(chooser * pair_epochs[None, :, 1], axis=1)
    epoch_number = jnp.arange(EPOCHS, dtype=jnp.int32)
    inside = (epoch_number[None, :] >= starts[:, None]) & (
        epoch_number[None, :] < finishes[:, None]
    )
    return inside.astype(jnp.float32)


def per_device(first_image, second_image, prior_motion, offsets, pair_epochs, pair_slot):
    band_rows = first_image.shape[1]
    columns = first_image.shape[2]
    margin = SEARCH + RADIUS
    stacked = jnp.concatenate((first_image, second_image), axis=0)
    extended = with_halo(stacked, (("rows", 1),), margin)
    extended = jnp.pad(extended, ((0, 0), (0, 0), (margin, margin)))
    first_padded = extended[
        0, SEARCH : SEARCH + band_rows + 2 * RADIUS, SEARCH : SEARCH + columns + 2 * RADIUS
    ]
    second_padded = extended[1]
    mean_first = box_sum(first_padded)
    var_first = box_sum(first_padded * first_padded) - mean_first * mean_first
    mean_second_all = box_sum(second_padded)
    square_second_all = box_sum(second_padded * second_padded)
    offset_blocks = offsets.reshape(OFFSETS // 8, 8, 2)
    pairs_count = lax.axis_size("pairs")
    pixels = band_rows * columns // pairs_count
    design_matrix = build_design(pair_epochs, pair_slot)
    normal_matrix = jnp.dot(design_matrix.T, design_matrix, precision=HIGHEST) + PENALTY * jnp.eye(
        EPOCHS, dtype=jnp.float32
    )
    inverse_matrix = invert_normal(normal_matrix)
    threshold = SPARSITY / PENALTY
    sparse = jnp.zeros((2, EPOCHS, pixels), jnp.float32)
    scaled = jnp.zeros((2, EPOCHS, pixels), jnp.float32)
    prior_band = prior_motion[:, 0]
    motion = prior_band
    for round_number in range(ROUNDS):

        def block_step(state_now, offset_block):
            running_max, weight_sum, sum_rows, sum_cols = state_now
            cross_correlation = jax.vmap(
                lambda shift_vector: correlate(
                    shift_vector,
                    first_padded,
                    second_padded,
                    mean_first,
                    var_first,
                    mean_second_all,
                    square_second_all,
                    band_rows,
                    columns,
                )
            )(offset_block)
            shifts = offset_block.astype(jnp.float32)
            pixel_distance = (shifts[:, 0, None, None] - prior_band[0]) ** 2 + (
                shifts[:, 1, None, None] - prior_band[1]
            ) ** 2
            match_scores = (cross_correlation - PRIOR_STRENGTH * pixel_distance) / SOFTMIN_HEAT
            new_max = jnp.maximum(running_max, jnp.max(match_scores, axis=0))
            rescale = jnp.exp(running_max - new_max)
            weights = jnp.exp(match_scores - new_max)
            weight_sum = weight_sum * rescale + jnp.sum(weights, axis=0)
            sum_rows = sum_rows * rescale + jnp.sum(weights * shifts[:, 0, None, None], axis=0)
            sum_cols = sum_cols * rescale + jnp.sum(weights * shifts[:, 1, None, None], axis=0)
            return ((new_max, weight_sum, sum_rows, sum_cols), None)

        zeros_band = jnp.zeros((band_rows, columns), jnp.float32)
        initial = (
            jnp.full((band_rows, columns), -jnp.inf, jnp.float32),
            zeros_band,
            zeros_band,
            zeros_band,
        )
        (running_max, weight_sum, sum_rows, sum_cols), unused = lax.scan(
            block_step, initial, offset_blocks
        )
        motion = jnp.stack((sum_rows / weight_sum, sum_cols / weight_sum))
        outgoing = motion.reshape(2, 1, pairs_count, pixels)
        arrived = lax.all_to_all(outgoing, "pairs", split_axis=2, concat_axis=1, tiled=True)
        observed = arrived.reshape(2, arrived.shape[1], pixels)
        fixed_part = jnp.einsum("pe,cpn->cen", design_matrix, observed, precision=HIGHEST)
        for iteration in range(ITERS):
            target = fixed_part + PENALTY * (sparse - scaled)
            estimate = jnp.einsum("ef,cfn->cen", inverse_matrix, target, precision=HIGHEST)
            blended = estimate + scaled
            sparse = blended - jnp.clip(blended, -threshold, threshold)
            scaled = blended - sparse
        if round_number + 1 < ROUNDS:
            predicted = jnp.einsum("pe,cen->cpn", design_matrix, sparse, precision=HIGHEST)
            predicted = predicted.reshape(2, predicted.shape[1], 1, pixels)
            returned = lax.all_to_all(predicted, "pairs", split_axis=1, concat_axis=2, tiled=True)
            prior_band = 0.5 * (prior_motion[:, 0] + returned.reshape(2, band_rows, columns))
    return (sparse[:, :, None, :], motion[:, None])


LANES = 128
SUBLANES = 8
GROUP = 16
UNROLL = 1
SPAN = 2 * SEARCH + 1
WINDOW = 2 * RADIUS + 1
LOG2E = 1.4426950408889634
SCALE = LOG2E / SOFTMIN_HEAT


def strip_rows(strip):
    tall = strip + 2 * RADIUS
    taller = strip + 2 * (SEARCH + RADIUS)
    return tall, taller, tall + taller + 2 * strip


def pack_kernel(first_in, second_in, prior_in, out, first, second, prior, arrivals):
    copies = [
        pltpu.make_async_copy(source, target, arrivals.at[k])
        for k, (source, target) in enumerate(((first_in, first), (second_in, second), (prior_in, prior)))
    ]
    for copy in copies:
        copy.start()
    band, columns = first.shape
    strip = SUBLANES
    tall, taller, per = strip_rows(strip)
    tiles = columns // LANES

    def windows(source, offset, reach, height):
        for block in range(band // strip):
            for tile in range(tiles):
                lanes = slice(tile * LANES, (tile + 1) * LANES)
                at = (block * tiles + tile) * per + offset
                low = block * strip - reach
                start, stop = max(low, 0), min(low + height, band)
                if start > low:
                    out[at : at + start - low, :] = jnp.zeros((start - low, LANES), jnp.float32)
                out[at + start - low : at + stop - low, :] = source[start:stop, lanes]
                if stop < low + height:
                    out[at + stop - low : at + height, :] = jnp.zeros((low + height - stop, LANES), jnp.float32)

    copies[0].wait()
    windows(first, 0, RADIUS, tall)
    copies[1].wait()
    windows(second, tall, SEARCH + RADIUS, taller)
    copies[2].wait()
    for component in range(2):
        windows(prior.at[component], tall + taller + component * strip, 0, strip)


def patch_kernel(other_first, other_second, packed, out, edge, departures):
    band, columns = other_first.shape
    strip = SUBLANES
    tall, taller, per = strip_rows(strip)
    tiles = columns // LANES
    blocks = band // strip
    here = lax.axis_index("rows")
    size = tiles * per
    last = blocks - 1
    rows_of = lambda block: pl.ds(pl.multiple_of(block * size, strip), size)
    copies = [
        pltpu.make_async_copy(
            packed.at[pl.ds(size, (blocks - 2) * size)], out.at[pl.ds(size, (blocks - 2) * size)], departures.at[0]
        ),
        pltpu.make_async_copy(packed.at[rows_of(here * last)], out.at[rows_of(here * last)], departures.at[1]),
    ]
    for copy in copies:
        copy.start()
    edge[...] = packed[rows_of((1 - here) * last), :]
    for tile in range(tiles):
        lanes = slice(tile * LANES, (tile + 1) * LANES)
        at = tile * per

        @pl.when(here > 0)
        def _():
            edge[at : at + RADIUS, :] = other_first[band - RADIUS :, lanes]
            edge[at + tall : at + tall + strip, :] = other_second[band - strip :, lanes]

        @pl.when(here == 0)
        def _():
            edge[at + tall - RADIUS : at + tall, :] = other_first[:RADIUS, lanes]
            edge[at + tall + taller - strip : at + tall + taller, :] = other_second[:strip, lanes]

    copies.append(pltpu.make_async_copy(edge, out.at[rows_of((1 - here) * last)], departures.at[2]))
    copies[2].start()
    for copy in copies:
        copy.wait()


def window_sums(rows):
    sums = []
    for top in range(0, len(rows) - WINDOW + 1, WINDOW - 1):
        size = min(WINDOW - 1, len(rows) - WINDOW + 1 - top)
        before = [rows[top + WINDOW - 2]]
        for row in range(WINDOW - 3, -1, -1):
            before.append(rows[top + row] + before[-1])
        before.reverse()
        after = rows[top + WINDOW - 1]
        for row in range(size):
            sums.append(before[row] + after)
            if row + 1 < size:
                after = after + rows[top + WINDOW + row]
    return sums


def split_rows(upper, lower):
    value = jnp.concatenate((upper, lower), axis=0)
    high = value.astype(jnp.bfloat16)
    rest = value - high.astype(jnp.float32)
    mid = rest.astype(jnp.bfloat16)
    low = (rest - mid.astype(jnp.float32)).astype(jnp.bfloat16)
    return high, mid, low


def lane_shift(tiles, edge, shift, lane):
    if shift > 0:
        tiles = [jnp.where(lane < shift, after, own) for own, after in zip(tiles, tiles[1:] + [edge])]
    elif shift < 0:
        tiles = [jnp.where(lane >= LANES + shift, before, own) for own, before in zip(tiles, [edge] + tiles[:-1])]
    else:
        return tiles
    return [pltpu.roll(tile, (-shift) % LANES, 1) for tile in tiles]


def plan_kernel(offsets, pair_epochs, pair_slot, inverse, lengths, table):
    count = pair_slot.shape[0]
    total = 2 * count
    cells = SPAN * SPAN

    ends = [pair_epochs[pair_slot[j], 0] for j in range(count)]
    ends += [pair_epochs[pair_slot[j], 1] for j in range(count)]
    ranks = [jnp.int32(0)] * total
    for a in range(total):
        for b in range(a + 1, total):
            ahead = (ends[a] <= ends[b]).astype(jnp.int32)
            ranks[b] = ranks[b] + ahead
            ranks[a] = ranks[a] + (1 - ahead)
    for a in range(total):
        table[a] = ranks[a]
        table[total + ranks[a]] = a
        table[2 * total + ranks[a]] = ends[a]
    for s in range(total - 1):
        width = (table[2 * total + s + 1] - table[2 * total + s]).astype(jnp.float32)
        lengths[s] = jnp.full((SUBLANES, LANES), width)

    gram = [[None] * count for _ in range(count)]
    for a in range(count):
        for b in range(a, count):
            shared = jnp.minimum(ends[count + a], ends[count + b]) - jnp.maximum(ends[a], ends[b])
            value = jnp.maximum(shared, 0).astype(jnp.float32) + (PENALTY if a == b else 0.0)
            gram[a][b] = gram[b][a] = jnp.full((SUBLANES, LANES), value)
    for k in range(count):
        pivot = 1.0 / gram[k][k]
        scaled = [gram[k][b] * pivot for b in range(count)]
        for a in range(count):
            if a == k:
                continue
            factor = gram[a][k]
            for b in range(count):
                if b != k:
                    gram[a][b] = gram[a][b] - factor * scaled[b]
            gram[a][k] = -(factor * pivot)
        for b in range(count):
            gram[k][b] = scaled[b]
        gram[k][k] = pivot
    for a in range(count):
        for b in range(count):
            inverse[a * count + b] = gram[a][b]

    first = 3 * total
    listed = first + cells - offsets.shape[0]

    def blank(cell, carry):
        table[listed + cell] = 0
        return carry

    lax.fori_loop(0, cells, blank, 0, unroll=9)

    def mark(k, carry):
        cell = (offsets[k, 1] + SEARCH) * SPAN + offsets[k, 0] + SEARCH
        table[listed + cell] = 1
        return carry

    lax.fori_loop(0, offsets.shape[0], mark, 0, unroll=8)

    def collect(cell, place):
        held = table[listed + cell]

        @pl.when(held == 0)
        def _():
            table[first + place] = cell

        return place + 1 - held

    lax.fori_loop(0, cells, collect, 0, unroll=3)


def prefix(lengths, values, running):
    total = jnp.zeros((SUBLANES, LANES), jnp.float32)
    running[0] = total
    for s, value in enumerate(values):
        total = total + lengths[s] * value
        running[s + 1] = total


def invert_round(count, fresh, observed, inverse, lengths, plan, sparse, spread, running, steps):
    groups = len(running)
    segments = 2 * count - 1
    threshold = SPARSITY / PENALTY

    def iterate(first):
        if not first:
            for group in range(groups):
                prefix(lengths, [spread[group, s] for s in range(segments)], running[group])
        for group in range(groups):
            residual = []
            for j in range(count):
                value = observed[pl.ds(group * SUBLANES * SUBLANES + j, SUBLANES, stride=SUBLANES), :]
                if not first:
                    value = value - (running[group][plan[count + j]] - running[group][plan[j]])
                residual.append(value)
            for a in range(count):
                terms = [inverse[a * count + b] * residual[b] for b in range(count)]
                while len(terms) > 1:
                    terms = [sum(terms[k : k + 2][1:], terms[k]) for k in range(0, len(terms), 2)]
                steps[group][a] = terms[0]
                steps[group][count + a] = -terms[0]
        for group in range(groups):
            level = None
            for s in range(segments):
                rise = steps[group][plan[2 * count + s]]
                level = rise if level is None else level + rise
                blended = level if first else sparse[group, s + 1] + level
                scaled = jnp.clip(blended, -threshold, threshold)
                shrunk = blended - scaled
                sparse[group, s + 1] = shrunk
                spread[group, s] = shrunk - scaled

    if fresh:
        iterate(True)

    def later(iteration, carry):
        iterate(False)
        return carry

    lax.fori_loop(1 if fresh else 0, ITERS, later, 0, unroll=UNROLL)


def velocity_kernel(matched, sparse_in, spread_in, inverse, lengths, plan, velocity, sparse, spread, *buffers):
    groups, held = sparse_in.shape[:2]
    segments = held - 2
    count = (segments + 1) // 2
    halves = groups // 2
    running, steps = buffers[:groups], buffers[groups:]
    bounds = 4 * count
    for group in range(groups):
        sparse[group] = sparse_in[group]
        spread[group] = spread_in[group]
    invert_round(count, False, matched, inverse, lengths, plan, sparse, spread, running, steps)

    def fill(low, high, s):
        values = [sparse[group, s] for group in range(groups)]

        def one(epoch, carry):
            for group in range(groups):
                half = group % halves
                velocity[group // halves, epoch, half * SUBLANES : (half + 1) * SUBLANES, :] = values[group]
            return carry

        lax.fori_loop(low, high, one, 0)

    fill(0, plan[bounds], 0)
    for s in range(segments):
        fill(plan[bounds + s], plan[bounds + s + 1], s + 1)
    fill(plan[bounds + segments], velocity.shape[1], segments + 1)


def signed_sums(terms):
    total = terms[SEARCH]
    moment = step = None
    for distance in range(SEARCH, 0, -1):
        below, above = terms[SEARCH - distance], terms[SEARCH + distance]
        total = total + (above + below)
        rise = above - below
        step = rise if step is None else step + rise
        moment = step if moment is None else moment + step
    return total, moment


def match(cells, first_guess, prior, predicted, table, matched):
    def pixel_tile(cell, carry):
        factors = []
        for component in range(2):
            value = prior[component * cells + cell]
            if not first_guess:
                at = pl.multiple_of((component * cells + cell) * SUBLANES, SUBLANES)
                value = 0.5 * (value + predicted[pl.ds(at, SUBLANES), :])
            nearest = jnp.clip(jnp.round(value), -float(SEARCH), float(SEARCH))
            centre = nearest * (0.5 * LOG2E * nearest - LOG2E * value)
            slope = LOG2E * value
            powers = {0: jnp.exp2(centre)}
            for shift in range(1, SEARCH + 1):
                level = centre - 0.5 * LOG2E * shift * shift
                rise = slope * float(shift)
                powers[shift] = jnp.exp2(level + rise)
                powers[-shift] = jnp.exp2(level - rise)
            factors.append([powers[shift] for shift in range(-SEARCH, SEARCH + 1)])
        weights, moments = [], []
        for column_shift in range(SPAN):
            total, moment = signed_sums(
                [
                    factors[0][row_shift] * table[(column_shift * SPAN + row_shift) * cells + cell]
                    for row_shift in range(SPAN)
                ]
            )
            weights.append(total * factors[1][column_shift])
            moments.append(moment * factors[1][column_shift])
        weight, column_moment = signed_sums(weights)
        row_moment = moments[0]
        for moment in moments[1:]:
            row_moment = row_moment + moment
        share = 1.0 / weight
        for component, value in enumerate((row_moment, column_moment)):
            at = pl.multiple_of((component * cells + cell) * SUBLANES, SUBLANES)
            matched[pl.ds(at, SUBLANES), :] = value * share
        return carry

    lax.fori_loop(0, cells, pixel_tile, 0, unroll=4)


def track_kernel(
    offsets,
    data,
    inverse,
    lengths,
    plan,
    motion,
    matched,
    sparse,
    spread,
    band,
    first,
    second,
    mean_first,
    scale_first,
    mean_second,
    scale_second,
    table,
    prior,
    predicted,
    *buffers,
):
    strip = SUBLANES
    margin = SEARCH + RADIUS
    tall = strip + 2 * RADIUS
    taller = strip + 2 * margin
    per = tall + taller + 2 * strip
    wide = strip + 2 * SEARCH
    area = float(WINDOW * WINDOW)
    count = motion.shape[0]
    columns = band.shape[1]
    tiles = columns // LANES
    cells = strip * tiles
    groups = sparse.shape[0]
    segments = 2 * count - 1
    running, steps = buffers[:groups], buffers[groups:]
    nothing = jnp.zeros((SUBLANES, LANES), jnp.float32)
    lane = lax.broadcasted_iota(jnp.int32, (SUBLANES, LANES), 1)

    def clear(index, carry):
        at = plan[6 * count + index] * cells
        for cell in range(cells):
            table[at + cell] = nothing
        return carry

    lax.fori_loop(0, SPAN * SPAN - offsets.shape[0], clear, 0)

    tap = lax.broadcasted_iota(jnp.int32, band.shape[1:], 0)
    column = lax.broadcasted_iota(jnp.int32, band.shape[1:], 1)
    outside = jnp.where(column < LANES // 2, column + columns, column - LANES)
    for place, centre in enumerate((column, jnp.where(column < LANES, outside, -columns))):
        band[place] = jnp.where(jnp.abs(tap - centre) <= RADIUS, 1.0, 0.0).astype(jnp.bfloat16)

    def fetch(row, tile):
        return data[pl.ds(tile * per + row, SUBLANES, stride=tiles * per), :]

    for component in range(2):
        for row in range(strip):
            for tile in range(tiles):
                prior[component * cells + row * tiles + tile] = fetch(tall + taller + component * strip + row, tile)

    images = [[fetch(row, tile) for row in range(tall)] for tile in range(tiles)]
    for tile in range(tiles):
        for row in range(tall):
            first[row * tiles + tile] = images[tile][row]
    chosen = [[fetch(tall + row, tile) for row in range(taller)] for tile in range(tiles)]

    def multiply(columns_of_sums, totals, loads):
        pieces = [[], [], []]
        for sums in columns_of_sums:
            split = [split_rows(sums[row], sums[row + 1]) for row in range(0, len(sums), 2)]
            for part in range(3):
                pieces[part].append(jnp.concatenate([parts[part] for parts in split], axis=0))
        for part in range(3):
            left = jnp.concatenate(pieces[part], axis=1)
            for total, load in zip(totals, loads):
                pltpu.matmul_acc_lhs(total, left, load_staged_rhs=load if part == 0 else None)

    def statistics(*totals):
        pltpu.matmul_push_rhs(band[0], 0, 0)
        pltpu.matmul_push_rhs(band[1], 0, 1)
        square = lambda field: [[row * row for row in rows] for rows in field]
        sums_of = lambda field: [window_sums(rows) for rows in field]
        for at, field in enumerate((images, square(images))):
            multiply(sums_of(field), totals[at : at + 1], (0 if at == 0 else None,))
        for at, field in enumerate((chosen, square(chosen))):
            multiply(
                sums_of(field), (totals[2 + at], totals[4 + at]), (None, 0 if at == 0 else None)
            )
        for row in range(taller):
            pieces = [chosen[tile][row] for tile in range(tiles)]
            for shift in range(-SEARCH, SEARCH + 1):
                moved = lane_shift(pieces, nothing, shift, lane)
                for tile in range(tiles):
                    second[((shift + SEARCH) * taller + row) * tiles + tile] = moved[tile]
        totals = [pltpu.matmul_pop(total) for total in totals]
        for row in range(strip):
            for tile in range(tiles):
                at = (slice(row * SUBLANES, (row + 1) * SUBLANES), slice(tile * LANES, (tile + 1) * LANES))
                mean = totals[0][at] / area
                variance = totals[1][at] / area - mean * mean
                mean_first[row * tiles + tile] = totals[0][at]
                scale_first[row * tiles + tile] = lax.rsqrt(
                    jnp.maximum(variance, VARIANCE_FLOOR)
                ) * (SCALE / area)
        for row in range(wide):
            means, scales = [], []
            rows = slice(row * SUBLANES, (row + 1) * SUBLANES)
            for tile in range(tiles + 1):
                source = 2 if tile < tiles else 4
                lanes = slice(tile % tiles * LANES, (tile % tiles + 1) * LANES)
                mean = totals[source][rows, lanes] / area
                variance = totals[source + 1][rows, lanes] / area - mean * mean
                means.append(mean)
                scales.append(lax.rsqrt(jnp.maximum(variance, VARIANCE_FLOOR)))
            for shift in range(-SEARCH, SEARCH + 1):
                for values, held in ((means, mean_second), (scales, scale_second)):
                    moved = lane_shift(values[:tiles], values[tiles], shift, lane)
                    for tile in range(tiles):
                        held[((shift + SEARCH) * wide + row) * tiles + tile] = moved[tile]

    pl.run_scoped(
        statistics,
        *[
            pltpu.ACC(unit)((rows * SUBLANES, columns), jnp.float32)
            for unit, rows in ((0, strip), (0, strip), (0, wide), (0, wide), (1, wide), (1, wide))
        ],
    )

    def place(k):
        return offsets[k, 0] + SEARCH, offsets[k, 1] + SEARCH

    def send(k, total, load):
        row_shift, column_shift = place(k)
        at_second = (column_shift * taller + row_shift) * tiles
        fields = []
        for tile in range(tiles):
            fields.append(
                window_sums(
                    [first[row * tiles + tile] * second[at_second + row * tiles + tile] for row in range(tall)]
                )
            )
        multiply(fields, (total,), (load,))

    def receive(k, total):
        row_shift, column_shift = place(k)
        at_second = (column_shift * wide + row_shift) * tiles
        at_table = (column_shift * SPAN + row_shift) * cells
        crossed = pltpu.matmul_pop(total)
        for row in range(strip):
            for tile in range(tiles):
                cell = row * tiles + tile
                value = crossed[row * SUBLANES : (row + 1) * SUBLANES, tile * LANES : (tile + 1) * LANES]
                covariance = value - mean_first[cell] * mean_second[at_second + cell]
                scaled = covariance * (scale_first[cell] * scale_second[at_second + cell])
                table[at_table + cell] = jnp.exp2(scaled)

    def all_offsets(*totals):
        pltpu.matmul_push_rhs(band[0], 0, 1)
        for member in range(GROUP):
            send(member, totals[member], 0 if member == 1 else None)

        def offset_group(group, carry):
            for member in range(GROUP):
                receive((group - 1) * GROUP + member, totals[member])
                send(group * GROUP + member, totals[member], None)
            return carry

        lax.fori_loop(1, offsets.shape[0] // GROUP, offset_group, 0)
        for member in range(GROUP):
            receive(offsets.shape[0] - GROUP + member, totals[member])

    pl.run_scoped(
        all_offsets,
        *[pltpu.ACC(member % 2)((strip * SUBLANES, columns), jnp.float32) for member in range(GROUP)],
    )

    for group in range(groups):
        sparse[group, 0] = nothing
        sparse[group, segments + 1] = nothing
    match(cells, True, prior, predicted, table, matched)
    for round_number in range(1, ROUNDS):
        invert_round(
            count, round_number == 1, matched, inverse, lengths, plan, sparse, spread, running, steps
        )
        for group in range(groups):
            prefix(lengths, [sparse[group, s + 1] for s in range(segments)], running[group])
            for j in range(count):
                predicted[pl.ds(group * SUBLANES * SUBLANES + j, SUBLANES, stride=SUBLANES), :] = (
                    running[group][plan[count + j]] - running[group][plan[j]]
                )
        match(cells, False, prior, predicted, table, matched)

    for j in range(count):
        for component in range(2):
            for tile in range(tiles):
                at = (component * cells + tile) * SUBLANES + j
                motion[j, component, :, tile * LANES : (tile + 1) * LANES] = matched[
                    pl.ds(at, SUBLANES, stride=tiles * SUBLANES), :
                ]


def by_strips(first_image, second_image, prior_motion, offsets, pair_epochs, pair_slot):
    band_rows, columns = first_image.shape[1:]
    margin = SEARCH + RADIUS
    count = lax.axis_size("pairs")
    strip = band_rows // count
    tiles = columns // LANES
    cells = strip * tiles
    tall = strip + 2 * RADIUS
    taller = strip + 2 * margin
    wide = strip + 2 * SEARCH
    per = tall + taller + 2 * strip
    vmem_spec = pl.BlockSpec(memory_space=pltpu.VMEM)
    images = (first_image[0], second_image[0])
    others = [lax.ppermute(image, "rows", [(0, 1), (1, 0)]) for image in images]
    message = (count * tiles * per, LANES)
    sources = [pltpu.with_memory_space_constraint(x, pltpu.HBM) for x in (*images, prior_motion[:, 0])]
    packed = pl.pallas_call(
        pack_kernel,
        out_shape=pltpu.VMEM(message, jnp.float32),
        in_specs=[pl.BlockSpec(memory_space=pltpu.HBM)] * 3,
        out_specs=vmem_spec,
        scratch_shapes=[pltpu.VMEM(x.shape, jnp.float32) for x in sources] + [pltpu.SemaphoreType.DMA((3,))],
        compiler_params=pltpu.CompilerParams(vmem_limit_bytes=4 * 1024 * 1024),
    )(*sources)
    packed = pl.pallas_call(
        patch_kernel,
        out_shape=pltpu.HBM(message, jnp.float32),
        in_specs=[vmem_spec] * 3,
        out_specs=pl.BlockSpec(memory_space=pltpu.HBM),
        scratch_shapes=[
            pltpu.VMEM((tiles * per, LANES), jnp.float32),
            pltpu.SemaphoreType.DMA((3,)),
        ],
        compiler_params=pltpu.CompilerParams(vmem_limit_bytes=4 * 1024 * 1024),
    )(*others, packed)
    arrived = lax.all_to_all(packed, "pairs", split_axis=0, concat_axis=0, tiled=True)
    tile = lambda *lead: pltpu.VMEM((*lead, SUBLANES, LANES), jnp.float32)
    shape = lambda *lead: jax.ShapeDtypeStruct((*lead, SUBLANES, LANES), jnp.float32)
    flat = jax.ShapeDtypeStruct((2 * cells * SUBLANES, LANES), jnp.float32)
    groups = 2 * cells // SUBLANES
    segments = 2 * count - 1
    smem = pl.BlockSpec(memory_space=pltpu.SMEM)
    vmem = pl.BlockSpec(memory_space=pltpu.VMEM)
    buffers = [tile(2 * count)] * groups + [tile(2 * count)] * groups
    entries = 6 * count + 2 * SPAN * SPAN - offsets.shape[0]
    inverse, lengths, plan = pl.pallas_call(
        plan_kernel,
        out_shape=(
            shape(count * count),
            shape(segments),
            jax.ShapeDtypeStruct((entries,), jnp.int32),
        ),
        in_specs=[smem] * 3,
        out_specs=(vmem, vmem, smem),
        compiler_params=pltpu.CompilerParams(vmem_limit_bytes=4 * 1024 * 1024),
    )(offsets, pair_epochs, pair_slot)
    motion, matched, sparse, spread = pl.pallas_call(
        track_kernel,
        out_shape=(
            jax.ShapeDtypeStruct((count, 2, strip, columns), jnp.float32),
            flat,
            shape(groups, segments + 2),
            shape(groups, segments),
        ),
        in_specs=[smem, vmem, vmem, vmem, smem],
        out_specs=(vmem, vmem, vmem, vmem),
        scratch_shapes=[
            pltpu.VMEM((2, columns, columns), jnp.bfloat16),
            tile(tall * tiles),
            tile(SPAN * taller * tiles),
            tile(cells),
            tile(cells),
            tile(SPAN * wide * tiles),
            tile(SPAN * wide * tiles),
            tile(SPAN * SPAN * cells),
            tile(2 * cells),
            pltpu.VMEM(flat.shape, jnp.float32),
            *buffers,
        ],
        compiler_params=pltpu.CompilerParams(vmem_limit_bytes=32 * 1024 * 1024),
    )(offsets, arrived, inverse, lengths, plan)
    velocity = pl.pallas_call(
        velocity_kernel,
        out_shape=jax.ShapeDtypeStruct((2, EPOCHS, cells, LANES), jnp.float32),
        in_specs=[vmem] * 5 + [smem],
        out_specs=vmem,
        scratch_shapes=[tile(groups, segments + 2), tile(groups, segments), *buffers],
        compiler_params=pltpu.CompilerParams(vmem_limit_bytes=16 * 1024 * 1024),
    )(matched, sparse, spread, inverse, lengths, plan)
    returned = lax.all_to_all(motion, "pairs", split_axis=0, concat_axis=0, tiled=True)
    returned = jnp.moveaxis(returned, 0, 1).reshape(2, 1, band_rows, columns)
    return (velocity.reshape(2, EPOCHS, 1, strip * columns), returned)


def per_device_any(first_image, second_image, *rest):
    band_rows, columns = first_image.shape[1:]
    count = lax.axis_size("pairs")
    strips = (
        count == SUBLANES
        and band_rows == count * SUBLANES
        and columns == 2 * LANES
        and lax.axis_size("rows") == 2
        and rest[1].shape[0] % GROUP == 0
    )
    plan = by_strips if strips else per_device
    return plan(first_image, second_image, *rest)


def solution(mesh):
    placed = (
        P(("groups", "pairs"), "rows", None),
        P(("groups", "pairs"), "rows", None),
        P(None, ("groups", "pairs"), "rows", None),
        P(),
        P("groups", None),
        P("groups"),
    )
    return jax.shard_map(
        per_device_any,
        mesh=mesh,
        in_specs=placed,
        out_specs=(
            P(None, None, ("groups", "rows"), "pairs"),
            P(None, ("groups", "pairs"), "rows", None),
        ),
        check_vma=False,
    )
```

```python
import functools

import jax
import jax.numpy as jnp
from jax import lax
from jax.experimental import pallas as pl
from jax.experimental.pallas import tpu as pltpu
from jax.sharding import PartitionSpec as P

OFFSETS = 64
SEARCH = 4
RADIUS = 4
EPOCHS = 128
ITERS = 4
ROUNDS = 2


SOFTMIN_HEAT = 0.1
PRIOR_STRENGTH = 0.05
PENALTY = 4.0
SPARSITY = 0.4
VARIANCE_FLOOR = 0.05
HIGHEST = lax.Precision.HIGHEST
NEWTON_STEPS = 32


def with_halo(cells, sides, width):
    for axis, dim in sides:
        count = lax.axis_size(axis)
        ends = count - 1
        head = lax.slice_in_dim(cells, 0, width, axis=dim)
        tail = lax.slice_in_dim(cells, cells.shape[dim] - width, cells.shape[dim], axis=dim)
        cells = jnp.concatenate(
            [
                lax.ppermute(tail, axis, [(i, (i + 1) % count) for i in range(ends)]),
                cells,
                lax.ppermute(head, axis, [((i + 1) % count, i) for i in range(ends)]),
            ],
            axis=dim,
        )
    return cells


def invert_normal(normal_matrix):
    order = normal_matrix.shape[0]
    identity = jnp.eye(order, dtype=jnp.float32)
    column_bound = jnp.max(jnp.sum(jnp.abs(normal_matrix), axis=0))
    estimate = identity / column_bound
    for step in range(NEWTON_STEPS):
        product = jnp.dot(normal_matrix, estimate, precision=HIGHEST)
        estimate = jnp.dot(estimate, 2.0 * identity - product, precision=HIGHEST)
    return estimate


def box_sum(values):
    window = 2 * RADIUS + 1
    height = values.shape[-2] - 2 * RADIUS
    breadth = values.shape[-1] - 2 * RADIUS
    running = values[..., 0:height, :]
    for position in range(1, window):
        running = running + values[..., position : position + height, :]
    summed = running[..., 0:breadth]
    for position in range(1, window):
        summed = summed + running[..., position : position + breadth]
    return summed / float(window * window)


def correlate(
    shift_vector,
    first_padded,
    second_padded,
    mean_first,
    var_first,
    mean_second_all,
    square_second_all,
    height,
    columns,
):
    row_start = shift_vector[0] + SEARCH
    col_start = shift_vector[1] + SEARCH
    mean_second = lax.dynamic_slice(mean_second_all, (row_start, col_start), (height, columns))
    square_second = lax.dynamic_slice(square_second_all, (row_start, col_start), (height, columns))
    window_second = lax.dynamic_slice(
        second_padded, (row_start, col_start), (height + 2 * RADIUS, columns + 2 * RADIUS)
    )
    covariance = box_sum(first_padded * window_second) - mean_first * mean_second
    var_second = square_second - mean_second * mean_second
    return covariance / jnp.sqrt(
        jnp.maximum(var_first, VARIANCE_FLOOR) * jnp.maximum(var_second, VARIANCE_FLOOR)
    )


def build_design(pair_epochs, pair_slot):
    pair_number = jnp.arange(pair_slot.shape[0], dtype=jnp.int32)
    chooser = (pair_slot[:, None] == pair_number[None, :]).astype(jnp.int32)
    starts = jnp.sum(chooser * pair_epochs[None, :, 0], axis=1)
    finishes = jnp.sum(chooser * pair_epochs[None, :, 1], axis=1)
    epoch_number = jnp.arange(EPOCHS, dtype=jnp.int32)
    inside = (epoch_number[None, :] >= starts[:, None]) & (
        epoch_number[None, :] < finishes[:, None]
    )
    return inside.astype(jnp.float32)


def per_device(first_image, second_image, prior_motion, offsets, pair_epochs, pair_slot):
    band_rows = first_image.shape[1]
    columns = first_image.shape[2]
    margin = SEARCH + RADIUS
    stacked = jnp.concatenate((first_image, second_image), axis=0)
    extended = with_halo(stacked, (("rows", 1),), margin)
    extended = jnp.pad(extended, ((0, 0), (0, 0), (margin, margin)))
    first_padded = extended[
        0, SEARCH : SEARCH + band_rows + 2 * RADIUS, SEARCH : SEARCH + columns + 2 * RADIUS
    ]
    second_padded = extended[1]
    mean_first = box_sum(first_padded)
    var_first = box_sum(first_padded * first_padded) - mean_first * mean_first
    mean_second_all = box_sum(second_padded)
    square_second_all = box_sum(second_padded * second_padded)
    offset_blocks = offsets.reshape(OFFSETS // 8, 8, 2)
    pairs_count = lax.axis_size("pairs")
    pixels = band_rows * columns // pairs_count
    design_matrix = build_design(pair_epochs, pair_slot)
    normal_matrix = jnp.dot(design_matrix.T, design_matrix, precision=HIGHEST) + PENALTY * jnp.eye(
        EPOCHS, dtype=jnp.float32
    )
    inverse_matrix = invert_normal(normal_matrix)
    threshold = SPARSITY / PENALTY
    sparse = jnp.zeros((2, EPOCHS, pixels), jnp.float32)
    scaled = jnp.zeros((2, EPOCHS, pixels), jnp.float32)
    prior_band = prior_motion[:, 0]
    motion = prior_band
    for round_number in range(ROUNDS):

        def block_step(state_now, offset_block):
            running_max, weight_sum, sum_rows, sum_cols = state_now
            cross_correlation = jax.vmap(
                lambda shift_vector: correlate(
                    shift_vector,
                    first_padded,
                    second_padded,
                    mean_first,
                    var_first,
                    mean_second_all,
                    square_second_all,
                    band_rows,
                    columns,
                )
            )(offset_block)
            shifts = offset_block.astype(jnp.float32)
            pixel_distance = (shifts[:, 0, None, None] - prior_band[0]) ** 2 + (
                shifts[:, 1, None, None] - prior_band[1]
            ) ** 2
            match_scores = (cross_correlation - PRIOR_STRENGTH * pixel_distance) / SOFTMIN_HEAT
            new_max = jnp.maximum(running_max, jnp.max(match_scores, axis=0))
            rescale = jnp.exp(running_max - new_max)
            weights = jnp.exp(match_scores - new_max)
            weight_sum = weight_sum * rescale + jnp.sum(weights, axis=0)
            sum_rows = sum_rows * rescale + jnp.sum(weights * shifts[:, 0, None, None], axis=0)
            sum_cols = sum_cols * rescale + jnp.sum(weights * shifts[:, 1, None, None], axis=0)
            return ((new_max, weight_sum, sum_rows, sum_cols), None)

        zeros_band = jnp.zeros((band_rows, columns), jnp.float32)
        initial = (
            jnp.full((band_rows, columns), -jnp.inf, jnp.float32),
            zeros_band,
            zeros_band,
            zeros_band,
        )
        (running_max, weight_sum, sum_rows, sum_cols), unused = lax.scan(
            block_step, initial, offset_blocks
        )
        motion = jnp.stack((sum_rows / weight_sum, sum_cols / weight_sum))
        outgoing = motion.reshape(2, 1, pairs_count, pixels)
        arrived = lax.all_to_all(outgoing, "pairs", split_axis=2, concat_axis=1, tiled=True)
        observed = arrived.reshape(2, arrived.shape[1], pixels)
        fixed_part = jnp.einsum("pe,cpn->cen", design_matrix, observed, precision=HIGHEST)
        for iteration in range(ITERS):
            target = fixed_part + PENALTY * (sparse - scaled)
            estimate = jnp.einsum("ef,cfn->cen", inverse_matrix, target, precision=HIGHEST)
            blended = estimate + scaled
            sparse = blended - jnp.clip(blended, -threshold, threshold)
            scaled = blended - sparse
        if round_number + 1 < ROUNDS:
            predicted = jnp.einsum("pe,cen->cpn", design_matrix, sparse, precision=HIGHEST)
            predicted = predicted.reshape(2, predicted.shape[1], 1, pixels)
            returned = lax.all_to_all(predicted, "pairs", split_axis=1, concat_axis=2, tiled=True)
            prior_band = 0.5 * (prior_motion[:, 0] + returned.reshape(2, band_rows, columns))
    return (sparse[:, :, None, :], motion[:, None])


LANES = 128
SUBLANES = 8
GROUP = 16
UNROLL = 1
SPAN = 2 * SEARCH + 1
WINDOW = 2 * RADIUS + 1
LOG2E = 1.4426950408889634
SCALE = LOG2E / SOFTMIN_HEAT


def strip_rows(strip):
    tall = strip + 2 * RADIUS
    taller = strip + 2 * (SEARCH + RADIUS)
    return tall, taller, tall + taller + 2 * strip


def pack_kernel(first_in, second_in, prior_in, out, first, second, prior, arrivals):
    copies = [
        pltpu.make_async_copy(source, target, arrivals.at[k])
        for k, (source, target) in enumerate(((first_in, first), (second_in, second), (prior_in, prior)))
    ]
    for copy in copies:
        copy.start()
    band, columns = first.shape
    strip = SUBLANES
    tall, taller, per = strip_rows(strip)
    tiles = columns // LANES

    def windows(source, offset, reach, height):
        for block in range(band // strip):
            for tile in range(tiles):
                lanes = slice(tile * LANES, (tile + 1) * LANES)
                at = (block * tiles + tile) * per + offset
                low = block * strip - reach
                start, stop = max(low, 0), min(low + height, band)
                if start > low:
                    out[at : at + start - low, :] = jnp.zeros((start - low, LANES), jnp.float32)
                out[at + start - low : at + stop - low, :] = source[start:stop, lanes]
                if stop < low + height:
                    out[at + stop - low : at + height, :] = jnp.zeros((low + height - stop, LANES), jnp.float32)

    copies[0].wait()
    windows(first, 0, RADIUS, tall)
    copies[1].wait()
    windows(second, tall, SEARCH + RADIUS, taller)
    copies[2].wait()
    for component in range(2):
        windows(prior.at[component], tall + taller + component * strip, 0, strip)


def patch_kernel(other_first, other_second, packed, out, edge, departures):
    band, columns = other_first.shape
    strip = SUBLANES
    tall, taller, per = strip_rows(strip)
    tiles = columns // LANES
    blocks = band // strip
    here = lax.axis_index("rows")
    size = tiles * per
    last = blocks - 1
    rows_of = lambda block: pl.ds(pl.multiple_of(block * size, strip), size)
    copies = [
        pltpu.make_async_copy(
            packed.at[pl.ds(size, (blocks - 2) * size)], out.at[pl.ds(size, (blocks - 2) * size)], departures.at[0]
        ),
        pltpu.make_async_copy(packed.at[rows_of(here * last)], out.at[rows_of(here * last)], departures.at[1]),
    ]
    for copy in copies:
        copy.start()
    edge[...] = packed[rows_of((1 - here) * last), :]
    for tile in range(tiles):
        lanes = slice(tile * LANES, (tile + 1) * LANES)
        at = tile * per

        @pl.when(here > 0)
        def _():
            edge[at : at + RADIUS, :] = other_first[band - RADIUS :, lanes]
            edge[at + tall : at + tall + strip, :] = other_second[band - strip :, lanes]

        @pl.when(here == 0)
        def _():
            edge[at + tall - RADIUS : at + tall, :] = other_first[:RADIUS, lanes]
            edge[at + tall + taller - strip : at + tall + taller, :] = other_second[:strip, lanes]

    copies.append(pltpu.make_async_copy(edge, out.at[rows_of((1 - here) * last)], departures.at[2]))
    copies[2].start()
    for copy in copies:
        copy.wait()


def window_sums(rows):
    sums = []
    for top in range(0, len(rows) - WINDOW + 1, WINDOW - 1):
        size = min(WINDOW - 1, len(rows) - WINDOW + 1 - top)
        before = [rows[top + WINDOW - 2]]
        for row in range(WINDOW - 3, -1, -1):
            before.append(rows[top + row] + before[-1])
        before.reverse()
        after = rows[top + WINDOW - 1]
        for row in range(size):
            sums.append(before[row] + after)
            if row + 1 < size:
                after = after + rows[top + WINDOW + row]
    return sums


def split_rows(upper, lower):
    value = jnp.concatenate((upper, lower), axis=0)
    high = value.astype(jnp.bfloat16)
    rest = value - high.astype(jnp.float32)
    mid = rest.astype(jnp.bfloat16)
    low = (rest - mid.astype(jnp.float32)).astype(jnp.bfloat16)
    return high, mid, low


def lane_shift(tiles, edge, shift, lane):
    if shift > 0:
        tiles = [jnp.where(lane < shift, after, own) for own, after in zip(tiles, tiles[1:] + [edge])]
    elif shift < 0:
        tiles = [jnp.where(lane >= LANES + shift, before, own) for own, before in zip(tiles, [edge] + tiles[:-1])]
    else:
        return tiles
    return [pltpu.roll(tile, (-shift) % LANES, 1) for tile in tiles]


def plan_kernel(offsets, pair_epochs, pair_slot, inverse, lengths, table):
    count = pair_slot.shape[0]
    total = 2 * count
    cells = SPAN * SPAN

    ends = [pair_epochs[pair_slot[j], 0] for j in range(count)]
    ends += [pair_epochs[pair_slot[j], 1] for j in range(count)]
    ranks = [jnp.int32(0)] * total
    for a in range(total):
        for b in range(a + 1, total):
            ahead = (ends[a] <= ends[b]).astype(jnp.int32)
            ranks[b] = ranks[b] + ahead
            ranks[a] = ranks[a] + (1 - ahead)
    for a in range(total):
        table[a] = ranks[a]
        table[total + ranks[a]] = a
        table[2 * total + ranks[a]] = ends[a]
    for s in range(total - 1):
        width = (table[2 * total + s + 1] - table[2 * total + s]).astype(jnp.float32)
        lengths[s] = jnp.full((SUBLANES, LANES), width)

    gram = [[None] * count for _ in range(count)]
    for a in range(count):
        for b in range(a, count):
            shared = jnp.minimum(ends[count + a], ends[count + b]) - jnp.maximum(ends[a], ends[b])
            value = jnp.maximum(shared, 0).astype(jnp.float32) + (PENALTY if a == b else 0.0)
            gram[a][b] = gram[b][a] = jnp.full((SUBLANES, LANES), value)
    for k in range(count):
        pivot = 1.0 / gram[k][k]
        scaled = [gram[k][b] * pivot for b in range(count)]
        for a in range(count):
            if a == k:
                continue
            factor = gram[a][k]
            for b in range(count):
                if b != k:
                    gram[a][b] = gram[a][b] - factor * scaled[b]
            gram[a][k] = -(factor * pivot)
        for b in range(count):
            gram[k][b] = scaled[b]
        gram[k][k] = pivot
    for a in range(count):
        for b in range(count):
            inverse[a * count + b] = gram[a][b]

    first = 3 * total
    listed = first + cells - offsets.shape[0]

    def blank(cell, carry):
        table[listed + cell] = 0
        return carry

    lax.fori_loop(0, cells, blank, 0, unroll=9)

    def mark(k, carry):
        cell = (offsets[k, 1] + SEARCH) * SPAN + offsets[k, 0] + SEARCH
        table[listed + cell] = 1
        return carry

    lax.fori_loop(0, offsets.shape[0], mark, 0, unroll=8)

    def collect(cell, place):
        held = table[listed + cell]

        @pl.when(held == 0)
        def _():
            table[first + place] = cell

        return place + 1 - held

    lax.fori_loop(0, cells, collect, 0, unroll=3)


def prefix(lengths, values, running):
    total = jnp.zeros((SUBLANES, LANES), jnp.float32)
    running[0] = total
    for s, value in enumerate(values):
        total = total + lengths[s] * value
        running[s + 1] = total


def invert_round(count, fresh, observed, inverse, lengths, plan, sparse, spread, running, steps):
    groups = len(running)
    segments = 2 * count - 1
    threshold = SPARSITY / PENALTY

    def iterate(first):
        if not first:
            for group in range(groups):
                prefix(lengths, [spread[group, s] for s in range(segments)], running[group])
        for group in range(groups):
            residual = []
            for j in range(count):
                value = observed[pl.ds(group * SUBLANES * SUBLANES + j, SUBLANES, stride=SUBLANES), :]
                if not first:
                    value = value - (running[group][plan[count + j]] - running[group][plan[j]])
                residual.append(value)
            for a in range(count):
                terms = [inverse[a * count + b] * residual[b] for b in range(count)]
                while len(terms) > 1:
                    terms = [sum(terms[k : k + 2][1:], terms[k]) for k in range(0, len(terms), 2)]
                steps[group][a] = terms[0]
                steps[group][count + a] = -terms[0]
        for group in range(groups):
            level = None
            for s in range(segments):
                rise = steps[group][plan[2 * count + s]]
                level = rise if level is None else level + rise
                blended = level if first else sparse[group, s + 1] + level
                scaled = jnp.clip(blended, -threshold, threshold)
                shrunk = blended - scaled
                sparse[group, s + 1] = shrunk
                spread[group, s] = shrunk - scaled

    if fresh:
        iterate(True)

    def later(iteration, carry):
        iterate(False)
        return carry

    lax.fori_loop(1 if fresh else 0, ITERS, later, 0, unroll=UNROLL)


def velocity_kernel(matched, sparse_in, spread_in, inverse, lengths, plan, velocity, sparse, spread, *buffers):
    groups, held = sparse_in.shape[:2]
    segments = held - 2
    count = (segments + 1) // 2
    halves = groups // 2
    running, steps = buffers[:groups], buffers[groups:]
    bounds = 4 * count
    for group in range(groups):
        sparse[group] = sparse_in[group]
        spread[group] = spread_in[group]
    invert_round(count, False, matched, inverse, lengths, plan, sparse, spread, running, steps)

    def fill(low, high, s):
        values = [sparse[group, s] for group in range(groups)]

        def one(epoch, carry):
            for group in range(groups):
                half = group % halves
                velocity[group // halves, epoch, half * SUBLANES : (half + 1) * SUBLANES, :] = values[group]
            return carry

        lax.fori_loop(low, high, one, 0)

    fill(0, plan[bounds], 0)
    for s in range(segments):
        fill(plan[bounds + s], plan[bounds + s + 1], s + 1)
    fill(plan[bounds + segments], velocity.shape[1], segments + 1)


def signed_sums(terms):
    total = terms[SEARCH]
    moment = step = None
    for distance in range(SEARCH, 0, -1):
        below, above = terms[SEARCH - distance], terms[SEARCH + distance]
        total = total + (above + below)
        rise = above - below
        step = rise if step is None else step + rise
        moment = step if moment is None else moment + step
    return total, moment


def match(cells, first_guess, prior, predicted, table, matched):
    def pixel_tile(cell, carry):
        factors = []
        for component in range(2):
            value = prior[component * cells + cell]
            if not first_guess:
                at = pl.multiple_of((component * cells + cell) * SUBLANES, SUBLANES)
                value = 0.5 * (value + predicted[pl.ds(at, SUBLANES), :])
            nearest = jnp.clip(jnp.round(value), -float(SEARCH), float(SEARCH))
            centre = nearest * (0.5 * LOG2E * nearest - LOG2E * value)
            slope = LOG2E * value
            powers = {0: jnp.exp2(centre)}
            for shift in range(1, SEARCH + 1):
                level = centre - 0.5 * LOG2E * shift * shift
                rise = slope * float(shift)
                powers[shift] = jnp.exp2(level + rise)
                powers[-shift] = jnp.exp2(level - rise)
            factors.append([powers[shift] for shift in range(-SEARCH, SEARCH + 1)])
        weights, moments = [], []
        for column_shift in range(SPAN):
            total, moment = signed_sums(
                [
                    factors[0][row_shift] * table[(column_shift * SPAN + row_shift) * cells + cell]
                    for row_shift in range(SPAN)
                ]
            )
            weights.append(total * factors[1][column_shift])
            moments.append(moment * factors[1][column_shift])
        weight, column_moment = signed_sums(weights)
        row_moment = moments[0]
        for moment in moments[1:]:
            row_moment = row_moment + moment
        share = 1.0 / weight
        for component, value in enumerate((row_moment, column_moment)):
            at = pl.multiple_of((component * cells + cell) * SUBLANES, SUBLANES)
            matched[pl.ds(at, SUBLANES), :] = value * share
        return carry

    lax.fori_loop(0, cells, pixel_tile, 0, unroll=4)


def track_kernel(
    offsets,
    data,
    inverse,
    lengths,
    plan,
    motion,
    matched,
    sparse,
    spread,
    band,
    first,
    second,
    mean_first,
    scale_first,
    mean_second,
    scale_second,
    table,
    prior,
    predicted,
    *buffers,
):
    strip = SUBLANES
    margin = SEARCH + RADIUS
    tall = strip + 2 * RADIUS
    taller = strip + 2 * margin
    per = tall + taller + 2 * strip
    wide = strip + 2 * SEARCH
    area = float(WINDOW * WINDOW)
    count = motion.shape[0]
    columns = band.shape[1]
    tiles = columns // LANES
    cells = strip * tiles
    groups = sparse.shape[0]
    segments = 2 * count - 1
    running, steps = buffers[:groups], buffers[groups:]
    nothing = jnp.zeros((SUBLANES, LANES), jnp.float32)
    lane = lax.broadcasted_iota(jnp.int32, (SUBLANES, LANES), 1)

    def clear(index, carry):
        at = plan[6 * count + index] * cells
        for cell in range(cells):
            table[at + cell] = nothing
        return carry

    for index in range(SPAN * SPAN - offsets.shape[0]):
        clear(index, 0)

    tap = lax.broadcasted_iota(jnp.int32, band.shape[1:], 0)
    column = lax.broadcasted_iota(jnp.int32, band.shape[1:], 1)
    outside = jnp.where(column < LANES // 2, column + columns, column - LANES)
    for place, centre in enumerate((column, jnp.where(column < LANES, outside, -columns))):
        band[place] = jnp.where(jnp.abs(tap - centre) <= RADIUS, 1.0, 0.0).astype(jnp.bfloat16)

    def fetch(row, tile):
        return data[pl.ds(tile * per + row, SUBLANES, stride=tiles * per), :]

    for component in range(2):
        for row in range(strip):
            for tile in range(tiles):
                prior[component * cells + row * tiles + tile] = fetch(tall + taller + component * strip + row, tile)

    images = [[fetch(row, tile) for row in range(tall)] for tile in range(tiles)]
    for tile in range(tiles):
        for row in range(tall):
            first[row * tiles + tile] = images[tile][row]
    chosen = [[fetch(tall + row, tile) for row in range(taller)] for tile in range(tiles)]

    def multiply(columns_of_sums, totals, loads):
        pieces = [[], [], []]
        for sums in columns_of_sums:
            split = [split_rows(sums[row], sums[row + 1]) for row in range(0, len(sums), 2)]
            for part in range(3):
                pieces[part].append(jnp.concatenate([parts[part] for parts in split], axis=0))
        for part in range(3):
            left = jnp.concatenate(pieces[part], axis=1)
            for total, load in zip(totals, loads):
                pltpu.matmul_acc_lhs(total, left, load_staged_rhs=load if part == 0 else None)

    def statistics(*totals):
        pltpu.matmul_push_rhs(band[0], 0, 0)
        pltpu.matmul_push_rhs(band[1], 0, 1)
        square = lambda field: [[row * row for row in rows] for rows in field]
        sums_of = lambda field: [window_sums(rows) for rows in field]
        for at, field in enumerate((images, square(images))):
            multiply(sums_of(field), totals[at : at + 1], (0 if at == 0 else None,))
        for at, field in enumerate((chosen, square(chosen))):
            multiply(
                sums_of(field), (totals[2 + at], totals[4 + at]), (None, 0 if at == 0 else None)
            )
        for row in range(taller):
            pieces = [chosen[tile][row] for tile in range(tiles)]
            for shift in range(-SEARCH, SEARCH + 1):
                moved = lane_shift(pieces, nothing, shift, lane)
                for tile in range(tiles):
                    second[((shift + SEARCH) * taller + row) * tiles + tile] = moved[tile]
        totals = [pltpu.matmul_pop(total) for total in totals]
        for row in range(strip):
            for tile in range(tiles):
                at = (slice(row * SUBLANES, (row + 1) * SUBLANES), slice(tile * LANES, (tile + 1) * LANES))
                mean = totals[0][at] / area
                variance = totals[1][at] / area - mean * mean
                mean_first[row * tiles + tile] = totals[0][at]
                scale_first[row * tiles + tile] = lax.rsqrt(
                    jnp.maximum(variance, VARIANCE_FLOOR)
                ) * (SCALE / area)
        for row in range(wide):
            means, scales = [], []
            rows = slice(row * SUBLANES, (row + 1) * SUBLANES)
            for tile in range(tiles + 1):
                source = 2 if tile < tiles else 4
                lanes = slice(tile % tiles * LANES, (tile % tiles + 1) * LANES)
                mean = totals[source][rows, lanes] / area
                variance = totals[source + 1][rows, lanes] / area - mean * mean
                means.append(mean)
                scales.append(lax.rsqrt(jnp.maximum(variance, VARIANCE_FLOOR)))
            for shift in range(-SEARCH, SEARCH + 1):
                for values, held in ((means, mean_second), (scales, scale_second)):
                    moved = lane_shift(values[:tiles], values[tiles], shift, lane)
                    for tile in range(tiles):
                        held[((shift + SEARCH) * wide + row) * tiles + tile] = moved[tile]

    pl.run_scoped(
        statistics,
        *[
            pltpu.ACC(unit)((rows * SUBLANES, columns), jnp.float32)
            for unit, rows in ((0, strip), (0, strip), (0, wide), (0, wide), (1, wide), (1, wide))
        ],
    )

    def place(k):
        return offsets[k, 0] + SEARCH, offsets[k, 1] + SEARCH

    def send(k, total, load):
        row_shift, column_shift = place(k)
        at_second = (column_shift * taller + row_shift) * tiles
        fields = []
        for tile in range(tiles):
            fields.append(
                window_sums(
                    [first[row * tiles + tile] * second[at_second + row * tiles + tile] for row in range(tall)]
                )
            )
        multiply(fields, (total,), (load,))

    def receive(k, total):
        row_shift, column_shift = place(k)
        at_second = (column_shift * wide + row_shift) * tiles
        at_table = (column_shift * SPAN + row_shift) * cells
        crossed = pltpu.matmul_pop(total)
        for row in range(strip):
            for tile in range(tiles):
                cell = row * tiles + tile
                value = crossed[row * SUBLANES : (row + 1) * SUBLANES, tile * LANES : (tile + 1) * LANES]
                covariance = value - mean_first[cell] * mean_second[at_second + cell]
                scaled = covariance * (scale_first[cell] * scale_second[at_second + cell])
                table[at_table + cell] = jnp.exp2(scaled)

    def all_offsets(*totals):
        pltpu.matmul_push_rhs(band[0], 0, 1)
        for member in range(GROUP):
            send(member, totals[member], 0 if member == 1 else None)

        def offset_group(group, carry):
            for member in range(GROUP):
                receive((group - 1) * GROUP + member, totals[member])
                send(group * GROUP + member, totals[member], None)
            return carry

        lax.fori_loop(1, offsets.shape[0] // GROUP, offset_group, 0)
        for member in range(GROUP):
            receive(offsets.shape[0] - GROUP + member, totals[member])

    pl.run_scoped(
        all_offsets,
        *[pltpu.ACC(member % 2)((strip * SUBLANES, columns), jnp.float32) for member in range(GROUP)],
    )

    for group in range(groups):
        sparse[group, 0] = nothing
        sparse[group, segments + 1] = nothing
    match(cells, True, prior, predicted, table, matched)
    for round_number in range(1, ROUNDS):
        invert_round(
            count, round_number == 1, matched, inverse, lengths, plan, sparse, spread, running, steps
        )
        for group in range(groups):
            prefix(lengths, [sparse[group, s + 1] for s in range(segments)], running[group])
            for j in range(count):
                predicted[pl.ds(group * SUBLANES * SUBLANES + j, SUBLANES, stride=SUBLANES), :] = (
                    running[group][plan[count + j]] - running[group][plan[j]]
                )
        match(cells, False, prior, predicted, table, matched)

    for j in range(count):
        for component in range(2):
            for tile in range(tiles):
                at = (component * cells + tile) * SUBLANES + j
                motion[j, component, :, tile * LANES : (tile + 1) * LANES] = matched[
                    pl.ds(at, SUBLANES, stride=tiles * SUBLANES), :
                ]


def by_strips(first_image, second_image, prior_motion, offsets, pair_epochs, pair_slot):
    band_rows, columns = first_image.shape[1:]
    margin = SEARCH + RADIUS
    count = lax.axis_size("pairs")
    strip = band_rows // count
    tiles = columns // LANES
    cells = strip * tiles
    tall = strip + 2 * RADIUS
    taller = strip + 2 * margin
    wide = strip + 2 * SEARCH
    per = tall + taller + 2 * strip
    vmem_spec = pl.BlockSpec(memory_space=pltpu.VMEM)
    images = (first_image[0], second_image[0])
    others = [lax.ppermute(image, "rows", [(0, 1), (1, 0)]) for image in images]
    message = (count * tiles * per, LANES)
    sources = [pltpu.with_memory_space_constraint(x, pltpu.HBM) for x in (*images, prior_motion[:, 0])]
    packed = pl.pallas_call(
        pack_kernel,
        out_shape=pltpu.VMEM(message, jnp.float32),
        in_specs=[pl.BlockSpec(memory_space=pltpu.HBM)] * 3,
        out_specs=vmem_spec,
        scratch_shapes=[pltpu.VMEM(x.shape, jnp.float32) for x in sources] + [pltpu.SemaphoreType.DMA((3,))],
        compiler_params=pltpu.CompilerParams(vmem_limit_bytes=4 * 1024 * 1024),
    )(*sources)
    packed = pl.pallas_call(
        patch_kernel,
        out_shape=pltpu.HBM(message, jnp.float32),
        in_specs=[vmem_spec] * 3,
        out_specs=pl.BlockSpec(memory_space=pltpu.HBM),
        scratch_shapes=[
            pltpu.VMEM((tiles * per, LANES), jnp.float32),
            pltpu.SemaphoreType.DMA((3,)),
        ],
        compiler_params=pltpu.CompilerParams(vmem_limit_bytes=4 * 1024 * 1024),
    )(*others, packed)
    arrived = lax.all_to_all(packed, "pairs", split_axis=0, concat_axis=0, tiled=True)
    tile = lambda *lead: pltpu.VMEM((*lead, SUBLANES, LANES), jnp.float32)
    shape = lambda *lead: jax.ShapeDtypeStruct((*lead, SUBLANES, LANES), jnp.float32)
    flat = jax.ShapeDtypeStruct((2 * cells * SUBLANES, LANES), jnp.float32)
    groups = 2 * cells // SUBLANES
    segments = 2 * count - 1
    smem = pl.BlockSpec(memory_space=pltpu.SMEM)
    vmem = pl.BlockSpec(memory_space=pltpu.VMEM)
    buffers = [tile(2 * count)] * groups + [tile(2 * count)] * groups
    entries = 6 * count + 2 * SPAN * SPAN - offsets.shape[0]
    inverse, lengths, plan = pl.pallas_call(
        plan_kernel,
        out_shape=(
            shape(count * count),
            shape(segments),
            jax.ShapeDtypeStruct((entries,), jnp.int32),
        ),
        in_specs=[smem] * 3,
        out_specs=(vmem, vmem, smem),
        compiler_params=pltpu.CompilerParams(vmem_limit_bytes=4 * 1024 * 1024),
    )(offsets, pair_epochs, pair_slot)
    motion, matched, sparse, spread = pl.pallas_call(
        track_kernel,
        out_shape=(
            jax.ShapeDtypeStruct((count, 2, strip, columns), jnp.float32),
            flat,
            shape(groups, segments + 2),
            shape(groups, segments),
        ),
        in_specs=[smem, vmem, vmem, vmem, smem],
        out_specs=(vmem, vmem, vmem, vmem),
        scratch_shapes=[
            pltpu.VMEM((2, columns, columns), jnp.bfloat16),
            tile(tall * tiles),
            tile(SPAN * taller * tiles),
            tile(cells),
            tile(cells),
            tile(SPAN * wide * tiles),
            tile(SPAN * wide * tiles),
            tile(SPAN * SPAN * cells),
            tile(2 * cells),
            pltpu.VMEM(flat.shape, jnp.float32),
            *buffers,
        ],
        compiler_params=pltpu.CompilerParams(vmem_limit_bytes=32 * 1024 * 1024),
    )(offsets, arrived, inverse, lengths, plan)
    velocity = pl.pallas_call(
        velocity_kernel,
        out_shape=jax.ShapeDtypeStruct((2, EPOCHS, cells, LANES), jnp.float32),
        in_specs=[vmem] * 5 + [smem],
        out_specs=vmem,
        scratch_shapes=[tile(groups, segments + 2), tile(groups, segments), *buffers],
        compiler_params=pltpu.CompilerParams(vmem_limit_bytes=16 * 1024 * 1024),
    )(matched, sparse, spread, inverse, lengths, plan)
    returned = lax.all_to_all(motion, "pairs", split_axis=0, concat_axis=0, tiled=True)
    returned = jnp.moveaxis(returned, 0, 1).reshape(2, 1, band_rows, columns)
    return (velocity.reshape(2, EPOCHS, 1, strip * columns), returned)


def per_device_any(first_image, second_image, *rest):
    band_rows, columns = first_image.shape[1:]
    count = lax.axis_size("pairs")
    strips = (
        count == SUBLANES
        and band_rows == count * SUBLANES
        and columns == 2 * LANES
        and lax.axis_size("rows") == 2
        and rest[1].shape[0] % GROUP == 0
    )
    plan = by_strips if strips else per_device
    return plan(first_image, second_image, *rest)


def solution(mesh):
    placed = (
        P(("groups", "pairs"), "rows", None),
        P(("groups", "pairs"), "rows", None),
        P(None, ("groups", "pairs"), "rows", None),
        P(),
        P("groups", None),
        P("groups"),
    )
    return jax.shard_map(
        per_device_any,
        mesh=mesh,
        in_specs=placed,
        out_specs=(
            P(None, None, ("groups", "rows"), "pairs"),
            P(None, ("groups", "pairs"), "rows", None),
        ),
        check_vma=False,
    )
```
